256 devices in a mesh: pipe: 2 (over core), dp: 128 (over x, y, z).
Axes of the slice: x: 4, y: 4, z: 8, core: 2. Of those that a mesh axis runs over, the one named last changes fastest.
Arguments:
- tokens: bfloat16 [4, 4096, 2048], P(None, 'dp'), may hold values from -40 to 40
- seg_ids: int32 [4, 4096], P(None, 'dp'), may hold values from 0 to 31, as said below
- cache_row: int32 [4, 4096], P(None, 'dp'), may hold values from 0 to 16383, as said below
- ln_gain: float32 [2, 2048], P('pipe'), may hold values from 0.1 to 1.9
- ln_bias: float32 [2, 2048], P('pipe'), may hold values from -2 to 2
- qkv_weight: bfloat16 [2, 2048, 3072], P('pipe', 'dp'), may hold values from -8 to 8
- qkv_bias: float32 [2, 3072], P('pipe'), may hold values from -3 to 3
- out_weight: bfloat16 [2, 1024, 2048], P('pipe', 'dp'), may hold values from -0.1875 to 0.1875
- out_bias: float32 [2, 2048], P('pipe'), may hold values from -2 to 2
Outputs:
- hidden: bfloat16 [2, 4, 4096, 2048], P('pipe', None, 'dp')
- kv_cache: bfloat16 [2, 16384, 2048], P('pipe', 'dp')
The draws below stay inside these ranges and needn't reach their ends.
Inputs may be any that keep to these rules, and one draw needn't show every extreme that they name: `seg_ids`: each block of 32 tokens of a micro-batch holds whole prompts, numbered from 0 in order, never crossing the block's edges. In every micro-batch one block holds a single prompt of 32 tokens and another holds 32 prompts of one token. `cache_row`: over all micro-batches each cache row is named once. Rows d * 4 * 32 to (d + 1) * 4 * 32 - 1 belong to index d of dp, which gets 32 of them in each micro-batch. Of the 32 tokens of one index of dp in one micro-batch, each owner gets none or exactly 2.
All inputs are finite; a program needn't handle non-finite values.
Results may differ from the reference program's by a relative error of at most 0.0065.
Values may be sent and summed in bfloat16 or wider, within the bound.
No kernel may reach another device: no remote copies, remote signals or barrier semaphores. Data moves between devices by JAX's collectives and lax.ppermute only.
A program may use at most 128 MiB of HBM per device.

```python
import jax
import jax.numpy as jnp
from jax import lax

D = 2048
HEADS = 4
HDIM = 256
ROT = 64
TOK_DEV = 32
MB = 4
LAYERS = 2
HW = 1024
TOKENS = 4096
CACHE = 16384
N_DP = 128


def draw_tokens(key, part):
    base_key = jax.random.fold_in(key, 0)
    base_rows = jax.random.normal(base_key, (MB, TOKENS, D), jnp.float32)
    return base_rows.astype(jnp.bfloat16)


def draw_seg_ids(key, part):
    device_count = TOKENS // TOK_DEV
    results = []
    micro_keys = jax.random.split(jax.random.fold_in(key, 17), MB)
    for micro_index in range(MB):
        rate_key, cut_key, pick_key = jax.random.split(micro_keys[micro_index], 3)
        rates = jax.random.randint(rate_key, (device_count, 1), 1, TOK_DEV + 1)
        cuts = (jax.random.randint(cut_key, (device_count, TOK_DEV), 0, TOK_DEV + 1) % rates == 0).astype(jnp.int32)
        chosen = jax.random.permutation(pick_key, device_count)
        device_ids = jnp.arange(device_count, dtype=jnp.int32)[:, None]
        cuts = jnp.where(device_ids == chosen[0], 0, cuts)
        cuts = jnp.where(device_ids == chosen[1], 1, cuts)
        cuts = cuts.at[:, 0].set(0)
        results.append(jnp.cumsum(cuts, axis=1).reshape(TOKENS))
    return jnp.stack(results).astype(jnp.int32)


def draw_qkv_weight(key, part):
    sub_keys = jax.random.split(key, 3)
    shape_one = (LAYERS, D, HW)
    query_part = jax.random.normal(sub_keys[0], shape_one, jnp.float32) * D ** (-0.5)
    key_part = jax.random.normal(sub_keys[1], shape_one, jnp.float32) * D ** (-0.5)
    value_part = jax.random.normal(sub_keys[2], shape_one, jnp.float32) * D ** (-0.5)
    return jnp.concatenate([query_part, key_part, value_part], axis=2).astype(jnp.bfloat16)


def draw_cache_row(key, part):
    device_count = TOKENS // TOK_DEV
    slot_cap = 2 * ((TOK_DEV + device_count - 1) // device_count)
    group_count = TOK_DEV // slot_cap
    owner_rows = MB * TOK_DEV
    sub_keys = jax.random.split(key, MB + 1)
    order_keys = jax.random.split(sub_keys[MB], device_count)
    within = jax.vmap(lambda one_key: jax.random.permutation(one_key, owner_rows))(order_keys)
    sources = jnp.arange(device_count, dtype=jnp.int32)[:, None]
    results = []
    for micro_index in range(MB):
        step_keys = jax.random.split(sub_keys[micro_index], 4)
        relabel_src = jax.random.permutation(step_keys[0], device_count)
        relabel_dst = jax.random.permutation(step_keys[1], device_count)
        offsets = jax.random.permutation(step_keys[2], device_count)[:group_count]
        token_keys = jax.random.split(step_keys[3], device_count)
        token_order = jax.vmap(lambda one_key: jax.random.permutation(one_key, TOK_DEV))(token_keys)
        group_of = token_order // slot_cap
        rank_of = token_order % slot_cap
        owner_of = relabel_dst[(relabel_src[:, None] + offsets[group_of]) % device_count]
        hit_table = jnp.zeros((device_count, device_count), jnp.int32).at[sources, owner_of].set(1)
        before = jnp.cumsum(hit_table, axis=0) - hit_table
        offset = before[sources, owner_of] * slot_cap + rank_of
        local_row = micro_index * TOK_DEV + offset
        global_row = owner_of * owner_rows + within[owner_of, local_row]
        results.append(global_row.reshape(TOKENS))
    return jnp.stack(results).astype(jnp.int32)


def levels(stream_key, dims, shards, least, top_value):
    def one(dim, blocks):
        heights = jax.random.uniform(jax.random.fold_in(jax.random.fold_in(stream_key, 6), dim), (blocks,), jnp.float32, least / len(shards), top_value / len(shards))
        return jnp.repeat(jnp.exp(heights), dims[dim] // blocks).reshape((-1,) + (1,) * (len(dims) - dim - 1))

    factor_of = one(*shards[0])
    for cut in shards[1:]:
        factor_of = factor_of * one(*cut)
    return factor_of


def scatter_about(key, shape, spread, bound, cuts=(), held_as=jnp.bfloat16):
    values = jax.random.normal(key, shape, jnp.float32) * spread
    if len(cuts) > 0:
        values = levels(key, shape, cuts, -0.22, 0.18) * values
    return jnp.clip(values, min=-bound, max=bound).astype(held_as)


def setup_inputs(seed: int = 0) -> dict:
    seeds = jax.random.split(jax.random.key(seed), 10)
    tokens = draw_tokens(jax.random.fold_in(seeds[9], 71), 0)
    seg_ids = draw_seg_ids(jax.random.fold_in(seeds[9], 71), 0)
    cache_row = draw_cache_row(jax.random.fold_in(seeds[9], 71), 0)
    ln_gain = jnp.clip(1.0 + 0.18 * jax.random.normal(seeds[3], (LAYERS, D), jnp.float32), 0.1, 1.9)
    ln_bias = scatter_about(seeds[4], (LAYERS, D), 0.3, 2.0, ((0, 2),), jnp.float32)
    qkv_weight = draw_qkv_weight(jax.random.fold_in(seeds[9], 71), 0)
    qkv_bias = scatter_about(seeds[6], (LAYERS, 3 * HW), 0.5, 3.0, ((0, 2),), jnp.float32)
    out_weight = scatter_about(seeds[7], (LAYERS, HW, D), HW ** -0.5, 0.1875, ((0, 2), (1, 128)))
    out_bias = scatter_about(seeds[8], (LAYERS, D), 0.3, 2.0, ((0, 2),), jnp.float32)
    return dict(tokens=tokens, seg_ids=seg_ids, cache_row=cache_row, ln_gain=ln_gain, ln_bias=ln_bias, qkv_weight=qkv_weight, qkv_bias=qkv_bias, out_weight=out_weight, out_bias=out_bias)


EPS = 1e-05

def layer_norm(layer_in, gain_row, shift_row):
    data = layer_in.astype(jnp.float32)
    centre = lax.optimization_barrier(jnp.mean(data, axis=-1, keepdims=True))
    centred = data - centre
    variance = lax.optimization_barrier(jnp.mean(centred * centred, axis=-1, keepdims=True))
    return (centred * lax.rsqrt(variance + EPS) * gain_row + shift_row).astype(jnp.bfloat16)

def rotary(projected, positions):
    row_count = projected.shape[0]
    shaped = projected.reshape(row_count, HEADS, HDIM)
    half_dims = ROT // 2
    inverse = 10000.0 ** (-2.0 * jnp.arange(half_dims, dtype=jnp.float32) / ROT)
    angles = positions.astype(jnp.float32)[:, None] * inverse[None, :]
    cosine = jnp.cos(angles)[:, None, :]
    sine_of = jnp.sin(angles)[:, None, :]
    leading = shaped[:, :, :half_dims]
    trailing = shaped[:, :, half_dims:ROT]
    turned = jnp.concatenate([leading * cosine - trailing * sine_of, trailing * cosine + leading * sine_of, shaped[:, :, ROT:]], axis=-1)
    return turned.reshape(row_count, HEADS * HDIM)

def positions_of(seg_row):
    blocks = seg_row.astype(jnp.int32).reshape(N_DP, TOK_DEV)
    earlier = lax.optimization_barrier(jnp.sum((blocks[:, None, :] < blocks[:, :, None]).astype(jnp.int32), axis=2))
    order = jnp.arange(TOK_DEV, dtype=jnp.int32)[None, :]
    return (order - earlier).astype(jnp.int32).reshape(TOKENS)

def attend(queries, key_rows, value_rows, seg_row):
    window = TOK_DEV
    head_scale = HDIM ** (-0.5)
    seg_row = seg_row.astype(jnp.int32)

    def one_block(block_index):
        start = (block_index * window).astype(jnp.int32)
        q_block = lax.dynamic_slice_in_dim(queries, start, window, 0).astype(jnp.float32).reshape(window, HEADS, HDIM)
        k_block = lax.dynamic_slice_in_dim(key_rows, start, window, 0).astype(jnp.float32).reshape(window, HEADS, HDIM)
        v_block = lax.dynamic_slice_in_dim(value_rows, start, window, 0).astype(jnp.float32).reshape(window, HEADS, HDIM)
        seg_block = lax.dynamic_slice_in_dim(seg_row, start, window, 0)
        order = jnp.arange(window, dtype=jnp.int32)
        allowed = (seg_block[:, None] == seg_block[None, :]) & (order[None, :] <= order[:, None])
        scores = jnp.einsum('qhd,khd->hqk', q_block, k_block) * head_scale
        scores = jnp.where(allowed[None], scores, -1e+30)
        row_top = lax.optimization_barrier(jnp.max(scores, axis=-1, keepdims=True))
        exp_scores = jnp.exp(scores - row_top)
        probabilities = (exp_scores / lax.optimization_barrier(jnp.sum(exp_scores, axis=-1, keepdims=True))).astype(jnp.bfloat16)
        context = jnp.einsum('hqk,khd->qhd', probabilities.astype(jnp.float32), v_block)
        return context.astype(jnp.bfloat16).reshape(window, HW)
    blocks = lax.map(one_block, jnp.arange(TOKENS // window, dtype=jnp.int32))
    return blocks.reshape(TOKENS, HW)

def reference(tokens, seg_ids, cache_row, ln_gain, ln_bias, qkv_weight, qkv_bias, out_weight, out_bias):
    positions = jnp.stack([positions_of(seg_ids[micro_index]) for micro_index in range(MB)])
    hidden_list = []
    cache_store = jnp.zeros((LAYERS, CACHE, 2 * HW), jnp.bfloat16)
    layer_in = tokens
    for layer_index in range(LAYERS):
        outputs = []
        for micro_index in range(MB):
            normed = layer_norm(layer_in[micro_index], ln_gain[layer_index], ln_bias[layer_index])
            projected = jnp.dot(normed, qkv_weight[layer_index], preferred_element_type=jnp.float32) + qkv_bias[layer_index]
            queries = rotary(projected[:, :HW], positions[micro_index]).astype(jnp.bfloat16)
            key_rows = rotary(projected[:, HW:2 * HW], positions[micro_index]).astype(jnp.bfloat16)
            value_rows = projected[:, 2 * HW:].astype(jnp.bfloat16)
            context = attend(queries, key_rows, value_rows, seg_ids[micro_index])
            layer_out = layer_in[micro_index].astype(jnp.float32) + jnp.dot(context, out_weight[layer_index], preferred_element_type=jnp.float32) + out_bias[layer_index]
            outputs.append(layer_out.astype(jnp.bfloat16))
            both_rows = jnp.concatenate([key_rows, value_rows], axis=1)
            cache_store = cache_store.at[layer_index, cache_row[micro_index].astype(jnp.int32)].set(both_rows)
        layer_in = jnp.stack(outputs)
        hidden_list.append(layer_in)
    return (jnp.stack(hidden_list), cache_store)
```

```python
import jax
import jax.numpy as jnp
from jax import lax
from jax.sharding import PartitionSpec as P

HEADS = 4
HDIM = 256
ROT = 64
HALF = ROT // 2
EPS = 1e-05
META = 128
BF = jnp.bfloat16
F32 = jnp.float32


def swap(value):
    return lax.ppermute(value, "pipe", [(0, 1), (1, 0)])


def mm(a, b):
    return jnp.dot(a, b, preferred_element_type=F32)


def layer_norm(layer_in, gain_row, shift_row):
    data = layer_in.astype(F32)
    centre = jnp.mean(data, axis=-1, keepdims=True)
    centred = data - centre
    variance = jnp.mean(centred * centred, axis=-1, keepdims=True)
    return (centred * lax.rsqrt(variance + EPS) * gain_row + shift_row).astype(BF)


def angles_of(positions):
    inverse = 10000.0 ** (-2.0 * jnp.arange(HALF, dtype=F32) / ROT)
    angles = positions[:, None] * inverse[None, :]
    return jnp.cos(angles), jnp.sin(angles)


def rotary(head_cols, cos_sin):
    cosine, sine = cos_sin
    out = []
    for first in range(0, head_cols.shape[1], HDIM):
        leading = head_cols[:, first : first + HALF]
        trailing = head_cols[:, first + HALF : first + ROT]
        out += [
            leading * cosine - trailing * sine,
            trailing * cosine + leading * sine,
            head_cols[:, first + ROT : first + HDIM],
        ]
    return jnp.concatenate(out, axis=-1)


def attend(queries, key_rows, value_rows, allowed):
    parts = []
    for first in range(0, queries.shape[1], HDIM):
        one = slice(first, first + HDIM)
        scores = lax.dot_general(
            queries[:, one], key_rows[:, one], (((1,), (1,)), ((), ())), preferred_element_type=F32
        ) * HDIM ** (-0.5)
        scores = jnp.where(allowed, scores, -1e30)
        exp_scores = jnp.exp(scores - jnp.max(scores, axis=-1, keepdims=True))
        probs = (exp_scores / jnp.sum(exp_scores, axis=-1, keepdims=True)).astype(BF)
        parts.append(mm(probs, value_rows[:, one]).astype(BF))
    return jnp.concatenate(parts, axis=-1)


def shards(
    tokens, seg_ids, cache_row, ln_gain, ln_bias, qkv_weight, qkv_bias, out_weight, out_bias
):
    micro_count, row_count, width = tokens.shape
    device_count = lax.axis_size("dp")
    core = lax.axis_index("pipe")
    first_core = core == 0
    cache_size = micro_count * row_count
    slot_cap = 2 * micro_count * ((row_count + device_count - 1) // device_count)
    head_width = qkv_weight.shape[2] // 3
    half_heads = head_width // 2
    half_width = width // 2

    def pick(a, b):
        return jnp.where(first_core, a, b)

    qkv_shard = qkv_weight[0].reshape(-1, 3, 2, half_heads)
    out_shard = out_weight[0]

    def packed(which):
        qkv_part = qkv_shard[:, :, which, :].reshape(-1, 3 * half_heads)
        out_part = out_shard[:, which * half_width : (which + 1) * half_width]
        out_part = jnp.concatenate(
            [out_part[:, : half_width // 2], out_part[:, half_width // 2 :]], axis=0
        )
        return jnp.concatenate([qkv_part, out_part], axis=1)

    low, high = packed(0), packed(1)
    kept = pick(low, high)
    got = swap(pick(high, low))
    both = jnp.concatenate([pick(kept, got), pick(got, kept)], axis=1)
    gathered = lax.all_gather(both, "dp", axis=0, tiled=True)

    vectors = jnp.concatenate([ln_gain[0], ln_bias[0], qkv_bias[0], out_bias[0]])
    vectors_got = swap(vectors)
    vectors_of = (pick(vectors, vectors_got), pick(vectors_got, vectors))

    def weights_of(layer):
        begin = layer * 2 * head_width
        qkv = gathered[:, begin : begin + 3 * half_heads]
        out = gathered[:, begin + 3 * half_heads : begin + 2 * head_width]
        out = out.reshape(device_count, 2, -1, half_heads)
        out = jnp.concatenate(
            [out[:, 0].reshape(head_width, half_heads), out[:, 1].reshape(head_width, half_heads)],
            axis=1,
        )
        other = swap(out)
        out = jnp.concatenate([pick(out, other), pick(other, out)], axis=1)
        vec = vectors_of[layer]
        gain = vec[:width]
        shift = vec[width : 2 * width]
        bias = vec[2 * width : 2 * width + 3 * head_width].reshape(3, 2, half_heads)
        bias = pick(bias[:, 0], bias[:, 1]).reshape(-1)
        out_b = vec[2 * width + 3 * head_width :]
        return qkv, bias, out, out_b, gain, shift

    flat = tokens.reshape(cache_size, width)
    seg = seg_ids.reshape(cache_size)
    rows = cache_row.reshape(cache_size)
    order = jnp.arange(cache_size, dtype=jnp.int32)
    micro = order // row_count
    same_micro = micro[:, None] == micro[None, :]
    positions = (order % row_count) - jnp.sum(
        (same_micro & (seg[None, :] < seg[:, None])).astype(jnp.int32), axis=1
    )
    earlier = order[None, :] <= order[:, None]
    allowed = same_micro & earlier & (seg[:, None] == seg[None, :])
    owners = rows // cache_size
    rank = jnp.sum(
        (same_micro & earlier & (owners[:, None] == owners[None, :])).astype(jnp.int32), axis=1
    ) - 1
    slot = owners * slot_cap + micro * (slot_cap // micro_count) + rank
    slots = device_count * slot_cap
    send = (jnp.arange(slots, dtype=jnp.int32)[:, None] == slot[None, :]).astype(BF)

    def exchange(payload):
        cols = payload.shape[1]
        filled = mm(send, payload).astype(BF).reshape(device_count, slot_cap, cols)
        arrived = lax.all_to_all(filled, "dp", split_axis=0, concat_axis=0, tiled=True)
        return arrived.reshape(slots, cols)

    lane = jnp.arange(META, dtype=jnp.int32)[None, :]
    meta = jnp.where(
        lane == 0,
        (rows % cache_size + 1)[:, None],
        jnp.where(lane == 1, positions[:, None], 0),
    ).astype(BF)
    half_tokens = pick(flat[:, :half_width], flat[:, half_width:])
    arrived = exchange(jnp.concatenate([half_tokens, meta], axis=1))
    place = arrived[:, half_width].astype(jnp.int32) - 1
    take = (order[:, None] == place[None, :]).astype(BF)
    own = mm(take, arrived).astype(BF)
    own_half = own[:, :half_width]
    own_other = swap(own_half)
    own_tokens = jnp.concatenate([pick(own_half, own_other), pick(own_other, own_half)], axis=1)
    turn = angles_of(positions.astype(F32))
    own_turn = angles_of(own[:, half_width + 1].astype(F32))

    def keys_values(layer_in, weights, cos_sin):
        qkv, bias, _, _, gain, shift = weights
        normed = layer_norm(layer_in, gain, shift)
        projected = mm(normed, qkv[:, half_heads:]) + bias[half_heads:]
        return jnp.concatenate(
            [rotary(projected[:, :half_heads], cos_sin), projected[:, half_heads:]], axis=1
        ).astype(BF)

    def context_of(layer_in, weights):
        qkv, bias, _, _, gain, shift = weights
        normed = layer_norm(layer_in, gain, shift)
        projected = mm(normed, qkv) + bias
        queries = rotary(projected[:, :half_heads], turn).astype(BF)
        key_rows = rotary(projected[:, half_heads : 2 * half_heads], turn).astype(BF)
        return attend(queries, key_rows, projected[:, 2 * half_heads :].astype(BF), allowed)

    def finish(layer_in, context_half, weights):
        other = swap(context_half)
        context = jnp.concatenate([pick(context_half, other), pick(other, context_half)], axis=1)
        return (layer_in.astype(F32) + mm(context, weights[2]) + weights[3]).astype(BF)

    layer0, layer1 = weights_of(0), weights_of(1)
    context0 = context_of(flat, layer0)
    own_context0 = mm(take, exchange(context0)).astype(BF)
    hidden0 = finish(flat, context0, layer0)
    own_kv0 = keys_values(own_tokens, layer0, own_turn)
    context1 = context_of(hidden0, layer1)
    hidden1 = finish(hidden0, context1, layer1)
    own_hidden0 = finish(own_tokens, own_context0, layer0)
    own_kv1 = keys_values(own_hidden0, layer1, own_turn)

    kept_kv = pick(own_kv0, own_kv1)
    got_kv = swap(pick(own_kv1, own_kv0))
    low_kv, high_kv = pick(kept_kv, got_kv), pick(got_kv, kept_kv)
    cache = jnp.concatenate(
        [
            low_kv[:, :half_heads],
            high_kv[:, :half_heads],
            low_kv[:, half_heads:],
            high_kv[:, half_heads:],
        ],
        axis=1,
    )
    hidden = pick(hidden0, hidden1).reshape(1, micro_count, row_count, width)
    return hidden, cache[None]


def solution(mesh):
    placed = (
        P(None, "dp", None),
        P(None, "dp"),
        P(None, "dp"),
        P("pipe", None),
        P("pipe", None),
        P("pipe", "dp", None),
        P("pipe", None),
        P("pipe", "dp", None),
        P("pipe", None),
    )
    return jax.shard_map(
        shards,
        mesh=mesh,
        in_specs=placed,
        out_specs=(P("pipe", None, "dp", None), P("pipe", "dp", None)),
        check_vma=False,
    )
```

```python
import functools

import jax
import jax.numpy as jnp
from jax import lax
from jax.experimental import pallas as pl
from jax.experimental.pallas import tpu as pltpu
from jax.sharding import Mesh
from jax.sharding import PartitionSpec as P

HDIM = 256
ROT = 64
HALF = ROT // 2
EPS = 1e-05
META = 128
LANES = 128
BF = jnp.bfloat16
F32 = jnp.float32
DP = ("x", "y", "z")
PLANE = ("x", "y")
CAP_Z = 48
CAP_P = 32


def swap(value):
    return lax.ppermute(value, "pipe", [(0, 1), (1, 0)])


def mm(a, b):
    return jnp.dot(a, b, preferred_element_type=F32)


def chooser(count, places):
    return (jnp.arange(count, dtype=jnp.int32)[:, None] == places[None, :]).astype(BF)


def slots_of(dest, valid, count, cap):
    rows = dest.shape[0]
    hits = ((dest[:, None] == jnp.arange(count, dtype=jnp.int32)[None, :]) & valid[:, None]).astype(BF)
    number = jnp.arange(rows, dtype=jnp.int32)
    before = mm((number[None, :] < number[:, None]).astype(BF), hits)
    rank = jnp.sum(before * hits.astype(F32), axis=1).astype(jnp.int32)
    fits = valid & (rank < cap)
    return jnp.where(fits, dest * cap + rank, -1), jnp.any(valid & (rank >= cap))


def with_sums(choice):
    return jnp.concatenate([choice, jnp.ones((8, choice.shape[1]), BF)], axis=0)


def across(filled, axes, cap):
    cols = filled.shape[1]
    arrived = lax.all_to_all(
        filled.reshape(-1, cap, cols), axes, split_axis=0, concat_axis=0, tiled=True
    )
    return arrived.reshape(-1, cols)


def turns_of(positions):
    lane = jnp.arange(LANES)
    inverse = 10000.0 ** (-2.0 * (lane % HALF).astype(F32) / ROT)
    angles = positions[:, None] * inverse[None, :]
    cosine, sine = jnp.cos(angles), jnp.sin(angles)
    rotated, first = (lane < ROT)[None, :], (lane < HALF)[None, :]
    return jnp.stack(
        [
            jnp.where(rotated, cosine, 1.0),
            jnp.where(first, -sine, 0.0),
            jnp.where(rotated & ~first, sine, 0.0),
        ]
    )


def layer_norm(layer_in, gain_row, shift_row):
    data = layer_in.astype(F32)
    centre = jnp.mean(data, axis=-1, keepdims=True)
    centred = data - centre
    variance = jnp.mean(centred * centred, axis=-1, keepdims=True)
    return (centred * lax.rsqrt(variance + EPS) * gain_row + shift_row).astype(BF)


def rotary(cols, turns):
    parts = []
    for first in range(0, cols.shape[1], HDIM):
        head = cols[:, first : first + LANES]
        parts.append(
            head * turns[0]
            + pltpu.roll(head, LANES - HALF, 1) * turns[1]
            + pltpu.roll(head, HALF, 1) * turns[2]
        )
        parts.append(cols[:, first + LANES : first + HDIM])
    return jnp.concatenate(parts, axis=1).astype(BF)


def attend(queries, key_rows, value_rows, allowed):
    parts = []
    for first in range(0, queries.shape[1], HDIM):
        one = slice(first, first + HDIM)
        scores = lax.dot_general(
            queries[:, one], key_rows[:, one], (((1,), (1,)), ((), ())), preferred_element_type=F32
        ) * HDIM ** (-0.5)
        scores = jnp.where(allowed > 0, scores, -1e30)
        exp_scores = jnp.exp(scores - jnp.max(scores, axis=-1, keepdims=True))
        probs = (exp_scores / jnp.sum(exp_scores, axis=-1, keepdims=True)).astype(BF)
        parts.append(mm(probs, value_rows[:, one]).astype(BF))
    return jnp.concatenate(parts, axis=1)


def conclude(projected, turns, allowed_ref, out_ref):
    turns = [turns[k] for k in range(3)]
    if allowed_ref is None:
        half = projected.shape[1] // 2
        out_ref[:, :half] = rotary(projected[:, :half], turns)
        out_ref[:, half:] = projected[:, half:].astype(BF)
    else:
        third = projected.shape[1] // 3
        queries = rotary(projected[:, :third], turns)
        key_rows = rotary(projected[:, third : 2 * third], turns)
        value_rows = projected[:, 2 * third :].astype(BF)
        out_ref[...] = attend(queries, key_rows, value_rows, allowed_ref[...])


def pieces_kernel(with_context, place, layer_in, gain, shift, bias, turns, *rest):
    allowed, rest = (rest[0], rest[1:]) if with_context else (None, rest)
    pieces, out_ref, normed = rest[:-2], rest[-2], rest[-1]
    whole = layer_norm(layer_in[...], gain[...], shift[...])
    for k in range(16):
        normed[k] = whole[:, k * LANES : (k + 1) * LANES]

    def left_hand(which, k, first, count):
        blocks = []
        for j in range(first, first + count):
            x_step, y_step = (k, j) if which == 0 else (j, k)
            x = lax.rem(place[0] + x_step, 4)
            y = lax.rem(place[1] + y_step, 4)
            blocks.append(normed[x * 4 + y])
        return jnp.concatenate(blocks, axis=1)

    sums = []
    number = 0
    for which in range(2):
        skip = 0 if with_context or which else 512
        total = None
        for k, first, count in ((0, 0, 4), (1, 0, 4), (3, 0, 4), (2, 0, 2), (2, 2, 2)):
            part = mm(left_hand(which, k, first, count), pieces[number][:, skip:])
            total = part if total is None else total + part
            number += 1
        sums.append(total)
    projected = jnp.concatenate(sums, axis=1) + bias[...]
    conclude(projected, turns, allowed, out_ref)


def whole_kernel(with_context, layer_in, gain, shift, bias, turns, *rest):
    allowed, rest = (rest[0], rest[1:]) if with_context else (None, rest)
    weights, out_ref, normed, total = rest[:-3], rest[-3], rest[-2], rest[-1]
    step = pl.program_id(0)
    depth = weights[0].shape[0]

    @pl.when(step == 0)
    def _():
        whole = layer_norm(layer_in[...], gain[...], shift[...])
        for k in range(normed.shape[0]):
            normed[k] = whole[:, k * depth : (k + 1) * depth]
        total[...] = jnp.broadcast_to(bias[...], total.shape)

    part = normed[step]
    first = 0
    for one in weights:
        width = one.shape[1]
        total[:, first : first + width] += mm(part, one[...])
        first += width

    @pl.when(step == pl.num_programs(0) - 1)
    def _():
        conclude(total[...], turns, allowed, out_ref)


def cost(rows, width, cols):
    return pl.CostEstimate(flops=rows * cols, bytes_accessed=rows * cols, transcendentals=0)


def project_pieces(place, layer_in, vectors, turns, allowed, pieces):
    rows, width = layer_in.shape
    gain, shift, bias = vectors
    with_context = allowed is not None
    out_cols = 512 if with_context else 1024
    if not with_context:
        bias = bias[:, 512:]
    operands = [layer_in, gain, shift, bias, turns, *((allowed,) if with_context else ()), *pieces]
    return pl.pallas_call(
        functools.partial(pieces_kernel, with_context),
        out_shape=jax.ShapeDtypeStruct((rows, out_cols), BF),
        in_specs=[pl.BlockSpec(memory_space=pltpu.SMEM)]
        + [pl.BlockSpec(memory_space=pltpu.VMEM)] * len(operands),
        out_specs=pl.BlockSpec(memory_space=pltpu.VMEM),
        scratch_shapes=[pltpu.VMEM((16, rows, LANES), BF)],
        cost_estimate=cost(rows, width, bias.shape[1]),
        compiler_params=pltpu.CompilerParams(vmem_limit_bytes=24 << 20),
    )(place, *operands)


def project_whole(layer_in, vectors, turns, allowed, gathered):
    rows, width = layer_in.shape
    gain, shift, bias = vectors
    with_context = allowed is not None
    out_cols = 512 if with_context else 1024
    if not with_context:
        bias = bias[:, 512:]
    operands = [layer_in, gain, shift, bias, turns, *((allowed,) if with_context else ())]
    depth = 512
    columns = (0, 1, 2) if with_context else (1, 2)
    return pl.pallas_call(
        functools.partial(whole_kernel, with_context),
        grid=(width // depth,),
        out_shape=jax.ShapeDtypeStruct((rows, out_cols), BF),
        in_specs=[
            pl.BlockSpec(one.shape, lambda k, rank=one.ndim: (0,) * rank) for one in operands
        ]
        + [pl.BlockSpec((depth, 512), lambda k, col=col: (k, col)) for col in columns],
        out_specs=pl.BlockSpec((rows, out_cols), lambda k: (0, 0)),
        scratch_shapes=[
            pltpu.VMEM((width // depth, rows, depth), BF),
            pltpu.VMEM((rows, bias.shape[1]), F32),
        ],
        cost_estimate=cost(rows, width, bias.shape[1]),
        compiler_params=pltpu.CompilerParams(vmem_limit_bytes=24 << 20),
    )(*operands, *[pltpu.with_memory_space_constraint(gathered, pltpu.HBM)] * len(columns))


def shifted(value, axis, by):
    size = lax.axis_size(axis)
    return lax.ppermute(value, axis, [(one, (one + by) % size) for one in range(size)])


def rings(blocks, axes, halves, later=()):
    size = lax.axis_size(axes[0])
    found = [{0: [block]} for block in blocks]
    ups = downs = list(blocks)
    for step in range(1, size // 2):
        ups = [shifted(up, axis, 1) for up, axis in zip(ups, axes)]
        downs = [shifted(down, axis, -1) for down, axis in zip(downs, axes)]
        ups, downs, later = lax.optimization_barrier((ups, downs, later))
        for one, up, down in zip(found, ups, downs):
            one[size - step], one[step] = [up], [down]
    for one, up, down, axis in zip(found, ups, downs, axes):
        rows = up.shape[0] // 2
        if halves:
            one[size // 2] = [shifted(up[:rows], axis, 1), shifted(down[rows:], axis, -1)]
        else:
            one[size // 2] = [shifted(up, axis, 1)]
    return [[one[k] for k in range(size)] for one in found], later


def column_of(shard, later):
    rows, size = shard.shape[0], lax.axis_size("z")
    (ring,), later = rings([shard], ["z"], False, later)
    ring = jnp.concatenate([one[0] for one in ring] * 2, axis=0)
    begin = (size - lax.axis_index("z")) % size * rows
    return lax.dynamic_slice_in_dim(ring, begin, size * rows, 0), later


def pieces_of(ring):
    half = ring.shape[1] // 2
    pair, _ = rings([ring[:, :half], ring[:, half:]], ["y", "x"], False)
    pair = [jnp.concatenate([one[0] for one in each], axis=0) for each in pair]
    pair = lax.optimization_barrier(pair)
    order = []
    for each in rings(pair, ["x", "y"], True)[0]:
        order += [*each[0], *each[1], *each[3], *each[2]]
    return order


def shards(
    tokens, seg_ids, cache_row, ln_gain, ln_bias, qkv_weight, qkv_bias, out_weight, out_bias
):
    micro_count, row_count, width = tokens.shape
    device_count = lax.axis_size(DP)
    first_core = lax.axis_index("pipe") == 0
    cache_size = micro_count * row_count
    slot_cap = 2 * micro_count * ((row_count + device_count - 1) // device_count)
    head_width = qkv_weight.shape[2] // 3
    part = head_width // 2
    half_width = width // 2

    def pick(a, b):
        return jnp.where(first_core, a, b)

    def joined(piece):
        other = swap(piece)
        return jnp.concatenate([pick(piece, other), pick(other, piece)], axis=1)

    def packed(which):
        cuts = [
            qkv_weight[0][:, kind * head_width + which * part : kind * head_width + (which + 1) * part]
            for kind in range(3)
        ]
        begin = which * half_width
        out_cut = jnp.concatenate(
            [out_weight[0][:, begin : begin + part], out_weight[0][:, begin + part : begin + 2 * part]],
            axis=0,
        )
        return jnp.concatenate([*cuts, out_cut], axis=1)

    low, high = packed(0), packed(1)
    kept = pick(low, high)
    got = swap(pick(high, low))
    shard0, shard1 = pick(kept, got), pick(got, kept)
    bulk = jnp.concatenate([shard1, shard0[:, 3 * part :]], axis=1)
    gathered = lax.all_gather(bulk, DP, axis=0, tiled=True)
    column, (seg_ids, cache_row, ln_gain) = column_of(
        shard0[:, : 3 * part], (seg_ids, cache_row, ln_gain)
    )

    vectors = jnp.concatenate([ln_gain[0], ln_bias[0], qkv_bias[0], out_bias[0]])
    vectors_got = swap(vectors)

    def vectors_of(layer):
        vec = pick(vectors, vectors_got) if layer == 0 else pick(vectors_got, vectors)
        rest = vec[2 * width :]
        bias = [
            pick(
                rest[kind * head_width : kind * head_width + part],
                rest[kind * head_width + part : (kind + 1) * head_width],
            )
            for kind in range(3)
        ]
        out_b = rest[3 * head_width :]
        rows = (vec[None, :width], vec[None, width : 2 * width], jnp.concatenate(bias)[None, :])
        return rows, pick(out_b[:half_width], out_b[half_width:])

    (rows0, out_bias0), (rows1, out_bias1) = vectors_of(0), vectors_of(1)

    flat = tokens.reshape(cache_size, width)
    seg = seg_ids.reshape(cache_size)
    rows = cache_row.reshape(cache_size)
    order = jnp.arange(cache_size, dtype=jnp.int32)
    micro = order // row_count
    same_micro = micro[:, None] == micro[None, :]
    positions = (order % row_count) - jnp.sum(
        (same_micro & (seg[None, :] < seg[:, None])).astype(jnp.int32), axis=1
    )
    earlier = order[None, :] <= order[:, None]
    allowed = (same_micro & earlier & (seg[:, None] == seg[None, :])).astype(F32)
    owners = rows // cache_size
    rank = jnp.sum(
        (same_micro & earlier & (owners[:, None] == owners[None, :])).astype(jnp.int32), axis=1
    ) - 1
    slot = owners * slot_cap + micro * (slot_cap // micro_count) + rank
    depth = lax.axis_size("z")
    lane = jnp.arange(META, dtype=jnp.int32)[None, :]
    meta = jnp.where(
        lane == 0,
        (rows % cache_size + 1)[:, None],
        jnp.where(lane == 1, positions[:, None], jnp.where(lane == 2, (owners // depth)[:, None], 0)),
    ).astype(BF)
    half_tokens = pick(flat[:, :half_width], flat[:, half_width:])
    payload = jnp.concatenate([half_tokens, meta], axis=1)
    flag_at = half_width + 3

    def flagged(filled, flag, at):
        mark = (jnp.arange(filled.shape[1]) == at).astype(BF)[None, :]
        return filled + flag.astype(BF) * mark

    slot_z, out_z = slots_of(owners % depth, rows >= 0, depth, CAP_Z)
    send_z = chooser(depth * CAP_Z, slot_z)
    filled = flagged(mm(send_z, payload).astype(BF), out_z, flag_at)
    place = jnp.stack([lax.axis_index("x"), lax.axis_index("y")]).astype(jnp.int32)
    turns = turns_of(positions.astype(F32))
    filled, column, turns, allowed, send_z, place, rows0 = lax.optimization_barrier(
        (filled, column, turns, allowed, send_z, place, rows0)
    )
    middle = across(filled, "z", CAP_Z)
    pieces = pieces_of(column)
    slot_p, out_p = slots_of(
        middle[:, half_width + 2].astype(jnp.int32),
        middle[:, half_width] > 0,
        device_count // depth,
        CAP_P,
    )
    slots_p = device_count // depth * CAP_P
    send_p = with_sums(chooser(slots_p, slot_p))
    ran_out = out_p | jnp.any(middle[:, flag_at] > 0)

    context0 = project_pieces(place, flat, rows0, turns, allowed, pieces)
    filled = jnp.where(ran_out, jnp.nan, mm(send_z, context0)).astype(BF)
    middle0 = across(filled, "z", CAP_Z)
    leg = jnp.concatenate([middle[:, :half_width], middle0, middle[:, half_width:]], axis=1)
    leg = mm(send_p, leg).astype(BF)
    ran_out = jnp.isnan(leg[slots_p, half_width].astype(F32))
    wide = half_width + part
    arrived = across(flagged(leg[:slots_p], ran_out, flag_at + part), PLANE, CAP_P)
    gathered, ran_out = lax.optimization_barrier((gathered, ran_out))

    def finish(half, context, out, out_b):
        done = jnp.concatenate([mm(context, one) for one in out], axis=1)
        done = (half.astype(F32) + done + out_b).astype(BF)
        return done, joined(done)

    def out_of(begin):
        cut = gathered[:, begin : begin + part].reshape(device_count, 2, -1, part)
        return [cut[:, k].reshape(head_width, part) for k in range(2)]

    out0, out1 = out_of(4 * part), out_of(3 * part)
    hidden0_half, hidden0 = finish(half_tokens, joined(context0), out0, out_bias0)
    context1 = project_whole(hidden0, rows1, turns, allowed, gathered)
    arrived, context1 = lax.optimization_barrier((arrived, context1))
    _, hidden1 = finish(hidden0_half, joined(context1), out1, out_bias1)

    def unpacked(came):
        take = with_sums(chooser(cache_size, came[:, wide].astype(jnp.int32) - 1))
        return mm(take, came).astype(BF)

    def straight():
        row = jnp.concatenate([half_tokens, context0, meta], axis=1)
        row = mm(chooser(device_count * slot_cap, slot), row).astype(BF)
        return unpacked(across(row, DP, slot_cap))

    own = unpacked(arrived)
    ran_out = ran_out | (own[cache_size, flag_at + part] > 0)
    own = lax.cond(ran_out, straight, lambda: own)[:cache_size]
    own_turns = turns_of(own[:, wide + 1].astype(F32))
    own_part = own[:, :wide]
    other = swap(own_part)
    lower, upper = pick(own_part, other), pick(other, own_part)
    own_tokens = jnp.concatenate([lower[:, :half_width], upper[:, :half_width]], axis=1)
    own_context0 = jnp.concatenate([lower[:, half_width:], upper[:, half_width:]], axis=1)
    own_kv0 = project_pieces(place, own_tokens, rows0, own_turns, None, pieces)
    _, own_hidden0 = finish(own[:, :half_width], own_context0, out0, out_bias0)
    own_kv1 = project_whole(own_hidden0, rows1, own_turns, None, gathered)

    kept_kv = pick(own_kv0, own_kv1)
    got_kv = swap(pick(own_kv1, own_kv0))
    low_kv, high_kv = pick(kept_kv, got_kv), pick(got_kv, kept_kv)
    cache = jnp.concatenate(
        [low_kv[:, :part], high_kv[:, :part], low_kv[:, part:], high_kv[:, part:]], axis=1
    )
    hidden = pick(hidden0, hidden1).reshape(1, micro_count, row_count, width)
    return hidden, cache[None]


def solution(mesh):
    torus = Mesh(mesh.devices.reshape(2, 4, 4, 8), ("pipe", *DP))
    placed = (
        P(None, DP, None),
        P(None, DP),
        P(None, DP),
        P("pipe", None),
        P("pipe", None),
        P("pipe", DP, None),
        P("pipe", None),
        P("pipe", DP, None),
        P("pipe", None),
    )
    return jax.shard_map(
        shards,
        mesh=torus,
        in_specs=placed,
        out_specs=(P("pipe", None, DP, None), P("pipe", DP, None)),
        check_vma=False,
    )
```

```python
import functools

import jax
import jax.numpy as jnp
from jax import lax
from jax.experimental import pallas as pl
from jax.experimental.pallas import tpu as pltpu
from jax.sharding import Mesh
from jax.sharding import PartitionSpec as P

HDIM = 256
ROT = 64
HALF = ROT // 2
EPS = 1e-05
META = 128
LANES = 128
TILE = 256
BF = jnp.bfloat16
F32 = jnp.float32
DP = ("x", "y", "z")
PLANE = ("x", "y")
CAP_Z = 48
CAP_P = 32


def swap(value):
    return lax.ppermute(value, "pipe", [(0, 1), (1, 0)])


def mm(a, b):
    return jnp.dot(a, b, preferred_element_type=F32)


def chooser(count, places):
    return (jnp.arange(count, dtype=jnp.int32)[:, None] == places[None, :]).astype(BF)


def slots_of(dest, valid, count, cap):
    rows = dest.shape[0]
    hits = ((dest[:, None] == jnp.arange(count, dtype=jnp.int32)[None, :]) & valid[:, None]).astype(BF)
    number = jnp.arange(rows, dtype=jnp.int32)
    before = mm((number[None, :] < number[:, None]).astype(BF), hits)
    rank = jnp.sum(before * hits.astype(F32), axis=1).astype(jnp.int32)
    fits = valid & (rank < cap)
    return jnp.where(fits, dest * cap + rank, -1), jnp.any(valid & (rank >= cap))


def across(filled, axes, cap):
    cols = filled.shape[1]
    arrived = lax.all_to_all(
        filled.reshape(-1, cap, cols), axes, split_axis=0, concat_axis=0, tiled=True
    )
    return arrived.reshape(-1, cols)


def turns_of(positions):
    lane = jnp.arange(LANES)
    inverse = 10000.0 ** (-2.0 * (lane % HALF).astype(F32) / ROT)
    angles = positions[:, None] * inverse[None, :]
    cosine, sine = jnp.cos(angles), jnp.sin(angles)
    rotated, first = (lane < ROT)[None, :], (lane < HALF)[None, :]
    return jnp.stack(
        [
            jnp.where(rotated, cosine, 1.0),
            jnp.where(first, -sine, 0.0),
            jnp.where(rotated & ~first, sine, 0.0),
        ]
    )


def layer_norm(layer_in, gain_row, shift_row):
    data = layer_in.astype(F32)
    centre = jnp.mean(data, axis=-1, keepdims=True)
    centred = data - centre
    variance = jnp.mean(centred * centred, axis=-1, keepdims=True)
    return (centred * lax.rsqrt(variance + EPS) * gain_row + shift_row).astype(BF)


def rotary(cols, turns):
    parts = []
    for first in range(0, cols.shape[1], HDIM):
        head = cols[:, first : first + LANES]
        parts.append(
            head * turns[0]
            + pltpu.roll(head, LANES - HALF, 1) * turns[1]
            + pltpu.roll(head, HALF, 1) * turns[2]
        )
        parts.append(cols[:, first + LANES : first + HDIM])
    return jnp.concatenate(parts, axis=1).astype(BF)


def attend(queries, key_rows, value_rows, allowed):
    parts = []
    for first in range(0, queries.shape[1], HDIM):
        one = slice(first, first + HDIM)
        scores = lax.dot_general(
            queries[:, one], key_rows[:, one], (((1,), (1,)), ((), ())), preferred_element_type=F32
        ) * HDIM ** (-0.5)
        scores = jnp.where(allowed > 0, scores, -1e30)
        exp_scores = jnp.exp(scores - jnp.max(scores, axis=-1, keepdims=True))
        probs = (exp_scores / jnp.sum(exp_scores, axis=-1, keepdims=True)).astype(BF)
        parts.append(mm(probs, value_rows[:, one]).astype(BF))
    return jnp.concatenate(parts, axis=1)


def conclude(projected, turns, allowed_ref, out_ref):
    turns = [turns[k] for k in range(3)]
    if allowed_ref is None:
        half = projected.shape[1] // 2
        out_ref[:, :half] = rotary(projected[:, :half], turns)
        out_ref[:, half:] = projected[:, half:].astype(BF)
    else:
        third = projected.shape[1] // 3
        queries = rotary(projected[:, :third], turns)
        key_rows = rotary(projected[:, third : 2 * third], turns)
        value_rows = projected[:, 2 * third :].astype(BF)
        out_ref[...] = attend(queries, key_rows, value_rows, allowed_ref[...])


NEAR = ((0, 0, 4), (1, 0, 4), (3, 0, 4))
FAR = ((2, 0, 2), (2, 2, 2))


def cut(whole, normed):
    for k in range(normed.shape[0]):
        normed[k] = whole[:, k * LANES : (k + 1) * LANES]


def add_pieces(place, normed, parts, pieces, base, total, skipped):
    def left_hand(which, k, first, count):
        blocks = []
        for j in range(first, first + count):
            x_step, y_step = (k, j) if which == 0 else (j, k)
            x = lax.rem(place[0] + x_step, 4)
            y = lax.rem(place[1] + y_step, 4)
            blocks.append(normed[x * 4 + y])
        return jnp.concatenate(blocks, axis=1)

    def tile(which, number):
        column = pl.ds(pl.multiple_of(number * TILE, TILE), TILE)
        of_ring = pieces[len(parts) * which : len(parts) * (which + 1)]
        target = pl.ds(pl.multiple_of((3 * which + number) * TILE - skipped, TILE), TILE)
        result = jnp.broadcast_to(base[:, target], (total.shape[0], TILE))
        for part, piece in zip(parts, of_ring):
            result = result + mm(left_hand(which, *part), piece[:, column])
        total[:, target] = result

    for which in range(2):
        pl.loop(0 if which else skipped // TILE, 3)(functools.partial(tile, which))


def near_kernel(place, layer_in, gain, shift, bias, *rest):
    pieces, total, normed = rest[:-2], rest[-2], rest[-1]
    cut(layer_norm(layer_in[...], gain[...], shift[...]), normed)
    add_pieces(place, normed, NEAR, pieces, bias, total, 0)


def far_kernel(place, normed, near, turns, allowed, *rest):
    pieces, out_ref, total = rest[:-2], rest[-2], rest[-1]
    add_pieces(place, normed, FAR, pieces, near, total, 0)
    conclude(total[...], turns, allowed, out_ref)


def own_kernel(place, layer_in, gain, shift, bias, turns, *rest):
    pieces, out_ref, normed, total = rest[:-3], rest[-3], rest[-2], rest[-1]
    cut(layer_norm(layer_in[...], gain[...], shift[...]), normed)
    add_pieces(place, normed, NEAR + FAR, pieces, bias, total, 2 * TILE)
    conclude(total[...], turns, None, out_ref)


def unpack_kernel(came, own, marks):
    blocks = came.shape[1] // LANES
    last = came[:, (blocks - 1) * LANES :].astype(F32)
    lane = lax.broadcasted_iota(jnp.int32, last.shape, 1)
    named = jnp.sum(jnp.where(lane == 0, last, 0.0), axis=1, keepdims=True)
    take = (lane.astype(F32) + 1.0 == named).astype(BF)
    for first in range(0, blocks * LANES, 4 * LANES):
        part = came[:, first : min(first + 4 * LANES, blocks * LANES)]
        own[:, first : first + part.shape[1]] = lax.dot_general(
            take, part, (((0,), (0,)), ((), ())), preferred_element_type=F32
        ).astype(BF)
    marks[...] = jnp.sum(came[:, 8 * LANES : 9 * LANES].astype(F32), axis=0, keepdims=True)


def whole_kernel(with_context, layer_in, gain, shift, bias, turns, *rest):
    allowed, rest = (rest[0], rest[1:]) if with_context else (None, rest)
    weights, out_ref, normed, total = rest[:-3], rest[-3], rest[-2], rest[-1]
    step = pl.program_id(0)
    depth = weights[0].shape[0]

    @pl.when(step == 0)
    def _():
        whole = layer_norm(layer_in[...], gain[...], shift[...])
        for k in range(normed.shape[0]):
            normed[k] = whole[:, k * depth : (k + 1) * depth]
        total[...] = jnp.broadcast_to(bias[...], total.shape)

    part = normed[step]
    first = 0
    for one in weights:
        width = one.shape[1]
        total[:, first : first + width] += mm(part, one[...])
        first += width

    @pl.when(step == pl.num_programs(0) - 1)
    def _():
        conclude(total[...], turns, allowed, out_ref)


def cost(rows, width, cols):
    return pl.CostEstimate(flops=rows * cols, bytes_accessed=rows * cols, transcendentals=0)


def call(kernel, place, operands, out_shape, scratch, columns):
    rows = 128
    in_specs = [pl.BlockSpec(memory_space=pltpu.VMEM)] * len(operands)
    if place is not None:
        operands = [place, *operands]
        in_specs = [pl.BlockSpec(memory_space=pltpu.SMEM), *in_specs]
    return pl.pallas_call(
        kernel,
        out_shape=out_shape,
        in_specs=in_specs,
        out_specs=jax.tree.map(lambda one: pl.BlockSpec(memory_space=pltpu.VMEM), out_shape),
        scratch_shapes=[pltpu.VMEM(*one) for one in scratch],
        cost_estimate=cost(rows, rows, columns),
        compiler_params=pltpu.CompilerParams(vmem_limit_bytes=24 << 20),
    )(*operands)


def of(shape, dtype):
    return jax.ShapeDtypeStruct(shape, dtype)


def context_by_pieces(place, layer_in, vectors, turns, allowed, pieces):
    rows = layer_in.shape[0]
    columns = vectors[2].shape[1]
    sums, blocks = of((rows, columns), F32), of((16, rows, LANES), BF)
    near = [*pieces[:3], *pieces[5:8]]
    far = [*pieces[3:5], *pieces[8:]]
    total, normed = call(near_kernel, place, [layer_in, *vectors, *near], (sums, blocks), [], columns)
    return call(
        far_kernel,
        place,
        [normed, total, turns, allowed, *far],
        of((rows, 512), BF),
        [((rows, columns), F32)],
        columns,
    )


def own_by_pieces(place, layer_in, vectors, turns, pieces):
    rows = layer_in.shape[0]
    gain, shift, bias = vectors
    bias = bias[:, 512:]
    return call(
        own_kernel,
        place,
        [layer_in, gain, shift, bias, turns, *pieces],
        of((rows, 1024), BF),
        [((16, rows, LANES), BF), ((rows, 1024), F32)],
        1024,
    )


def project_whole(layer_in, vectors, turns, allowed, gathered):
    rows, width = layer_in.shape
    gain, shift, bias = vectors
    with_context = allowed is not None
    out_cols = 512 if with_context else 1024
    if not with_context:
        bias = bias[:, 512:]
    operands = [layer_in, gain, shift, bias, turns, *((allowed,) if with_context else ())]
    depth = 512
    columns = (0, 1, 2) if with_context else (1, 2)
    return pl.pallas_call(
        functools.partial(whole_kernel, with_context),
        grid=(width // depth,),
        out_shape=jax.ShapeDtypeStruct((rows, out_cols), BF),
        in_specs=[
            pl.BlockSpec(one.shape, lambda k, rank=one.ndim: (0,) * rank) for one in operands
        ]
        + [pl.BlockSpec((depth, 512), lambda k, col=col: (k, col)) for col in columns],
        out_specs=pl.BlockSpec((rows, out_cols), lambda k: (0, 0)),
        scratch_shapes=[
            pltpu.VMEM((width // depth, rows, depth), BF),
            pltpu.VMEM((rows, bias.shape[1]), F32),
        ],
        cost_estimate=cost(rows, width, bias.shape[1]),
        compiler_params=pltpu.CompilerParams(vmem_limit_bytes=24 << 20),
    )(*operands, *[pltpu.with_memory_space_constraint(gathered, pltpu.HBM)] * len(columns))


def shifted(value, axis, by):
    size = lax.axis_size(axis)
    return lax.ppermute(value, axis, [(one, (one + by) % size) for one in range(size)])


def rings(blocks, axes, halves):
    size = lax.axis_size(axes[0])
    found = [{0: [block]} for block in blocks]
    ups = downs = list(blocks)
    for step in range(1, size // 2):
        ups = [shifted(up, axis, 1) for up, axis in zip(ups, axes)]
        downs = [shifted(down, axis, -1) for down, axis in zip(downs, axes)]
        ups, downs = lax.optimization_barrier((ups, downs))
        for one, up, down in zip(found, ups, downs):
            one[size - step], one[step] = [up], [down]
    for one, up, down, axis in zip(found, ups, downs, axes):
        rows = up.shape[0] // 2
        if halves:
            one[size // 2] = [shifted(up[:rows], axis, 1), shifted(down[rows:], axis, -1)]
        else:
            one[size // 2] = [shifted(up, axis, 1)]
    return [[one[k] for k in range(size)] for one in found]


def column_of(shard, later):
    size, index = lax.axis_size("z"), lax.axis_index("z")
    block, step = shard[None], size // 2
    while step:
        got = lax.ppermute(block, "z", [(one, one ^ step) for one in range(size)])
        upper = (index // step) % 2 == 1
        both = [jnp.where(upper, got, block), jnp.where(upper, block, got)]
        block = jnp.stack(both, axis=1).reshape(-1, *shard.shape)
        if step == size // 2:
            block, later = lax.optimization_barrier((block, later))
        step //= 2
    return block.reshape(-1, shard.shape[1]), later


def pieces_of(ring):
    half = ring.shape[1] // 2
    pair = rings([ring[:, :half], ring[:, half:]], ["y", "x"], False)
    pair = [jnp.concatenate([one[0] for one in each], axis=0) for each in pair]
    pair = lax.optimization_barrier(pair)
    order = []
    for each in rings(pair, ["x", "y"], True):
        order += [*each[0], *each[1], *each[3], *each[2]]
    return order


def shards(
    tokens, seg_ids, cache_row, ln_gain, ln_bias, qkv_weight, qkv_bias, out_weight, out_bias
):
    micro_count, row_count, width = tokens.shape
    device_count = lax.axis_size(DP)
    first_core = lax.axis_index("pipe") == 0
    cache_size = micro_count * row_count
    slot_cap = 2 * micro_count * ((row_count + device_count - 1) // device_count)
    head_width = qkv_weight.shape[2] // 3
    part = head_width // 2
    half_width = width // 2

    def pick(a, b):
        return jnp.where(first_core, a, b)

    def joined(piece):
        other = swap(piece)
        return jnp.concatenate([pick(piece, other), pick(other, piece)], axis=1)

    def packed(which):
        cuts = [
            qkv_weight[0][:, kind * head_width + which * part : kind * head_width + (which + 1) * part]
            for kind in range(3)
        ]
        begin = which * half_width
        out_cut = jnp.concatenate(
            [out_weight[0][:, begin : begin + part], out_weight[0][:, begin + part : begin + 2 * part]],
            axis=0,
        )
        return jnp.concatenate([*cuts, out_cut], axis=1)

    low, high = packed(0), packed(1)
    kept = pick(low, high)
    got = swap(pick(high, low))
    shard0, shard1 = pick(kept, got), pick(got, kept)
    bulk = jnp.concatenate([shard1, shard0[:, 3 * part :]], axis=1)
    gathered = lax.all_gather(bulk, DP, axis=0, tiled=True)
    column, (seg_ids, cache_row, ln_gain) = column_of(
        shard0[:, : 3 * part], (seg_ids, cache_row, ln_gain)
    )

    vectors = jnp.concatenate([ln_gain[0], ln_bias[0], qkv_bias[0], out_bias[0]])
    vectors_got = swap(vectors)

    def vectors_of(layer):
        vec = pick(vectors, vectors_got) if layer == 0 else pick(vectors_got, vectors)
        rest = vec[2 * width :]
        bias = [
            pick(
                rest[kind * head_width : kind * head_width + part],
                rest[kind * head_width + part : (kind + 1) * head_width],
            )
            for kind in range(3)
        ]
        out_b = rest[3 * head_width :]
        rows = (vec[None, :width], vec[None, width : 2 * width], jnp.concatenate(bias)[None, :])
        return rows, pick(out_b[:half_width], out_b[half_width:])

    (rows0, out_bias0), (rows1, out_bias1) = vectors_of(0), vectors_of(1)

    flat = tokens.reshape(cache_size, width)
    seg = seg_ids.reshape(cache_size)
    rows = cache_row.reshape(cache_size)
    order = jnp.arange(cache_size, dtype=jnp.int32)
    micro = order // row_count
    same_micro = micro[:, None] == micro[None, :]
    positions = (order % row_count) - jnp.sum(
        (same_micro & (seg[None, :] < seg[:, None])).astype(jnp.int32), axis=1
    )
    earlier = order[None, :] <= order[:, None]
    allowed = (same_micro & earlier & (seg[:, None] == seg[None, :])).astype(F32)
    owners = rows // cache_size
    rank = jnp.sum(
        (same_micro & earlier & (owners[:, None] == owners[None, :])).astype(jnp.int32), axis=1
    ) - 1
    slot = owners * slot_cap + micro * (slot_cap // micro_count) + rank
    depth = lax.axis_size("z")
    lane = jnp.arange(META, dtype=jnp.int32)[None, :]
    meta = jnp.where(
        lane == 0,
        (rows % cache_size + 1)[:, None],
        jnp.where(lane == 1, positions[:, None], jnp.where(lane == 2, (owners // depth)[:, None], 0)),
    ).astype(BF)
    half_tokens = pick(flat[:, :half_width], flat[:, half_width:])
    payload = jnp.concatenate([half_tokens, meta], axis=1)
    flag_at = half_width + 3

    def flagged(filled, flag, at):
        mark = (jnp.arange(filled.shape[1]) == at).astype(BF)[None, :]
        return filled + flag.astype(BF) * mark

    slot_z, out_z = slots_of(owners % depth, rows >= 0, depth, CAP_Z)
    send_z = chooser(depth * CAP_Z, slot_z)
    filled = flagged(mm(send_z, payload).astype(BF), out_z, flag_at)
    place = jnp.stack([lax.axis_index("x"), lax.axis_index("y")]).astype(jnp.int32)
    turns = turns_of(positions.astype(F32))
    filled, column, turns, allowed, send_z, place, rows0 = lax.optimization_barrier(
        (filled, column, turns, allowed, send_z, place, rows0)
    )
    middle = across(filled, "z", CAP_Z)
    pieces = pieces_of(column)
    slot_p, out_p = slots_of(
        middle[:, half_width + 2].astype(jnp.int32),
        middle[:, half_width] > 0,
        device_count // depth,
        CAP_P,
    )
    slots_p = device_count // depth * CAP_P
    send_p = chooser(slots_p, slot_p)
    ran_out = out_p | jnp.any(middle[:, flag_at] > 0)

    context0 = context_by_pieces(place, flat, rows0, turns, allowed, pieces)
    filled = jnp.where(ran_out, jnp.nan, mm(send_z, context0)).astype(BF)
    middle0 = across(filled, "z", CAP_Z)
    leg = jnp.concatenate([middle[:, :half_width], middle0, middle[:, half_width:]], axis=1)
    leg = mm(send_p, leg).astype(BF)
    wide = half_width + part
    arrived = across(leg, PLANE, CAP_P)
    gathered, leg_mark = lax.optimization_barrier((gathered, leg[0, half_width]))

    def finish(half, context, out, out_b):
        done = jnp.concatenate([mm(context, one) for one in out], axis=1)
        done = (half.astype(F32) + done + out_b).astype(BF)
        return done, joined(done)

    def out_of(begin):
        cut = gathered[:, begin : begin + part].reshape(device_count, 2, -1, part)
        return [cut[:, k].reshape(head_width, part) for k in range(2)]

    out0, out1 = out_of(4 * part), out_of(3 * part)
    hidden0_half, hidden0 = finish(half_tokens, joined(context0), out0, out_bias0)
    context1 = project_whole(hidden0, rows1, turns, allowed, gathered)
    arrived, context1 = lax.optimization_barrier((arrived, context1))
    _, hidden1 = finish(hidden0_half, joined(context1), out1, out_bias1)

    def places(came_meta):
        return came_meta[:, 0].astype(jnp.int32) - 1

    def straight():
        row = jnp.concatenate([half_tokens, context0, meta], axis=1)
        fill = chooser(device_count * slot_cap, slot)
        blocks = row.shape[1] // META

        def some_columns(step, state):
            take, own = state
            begin = (blocks - 1 - step) * META
            part_of = lax.dynamic_slice_in_dim(row, begin, META, 1)
            came = across(mm(fill, part_of).astype(BF), DP, slot_cap)
            take = jnp.where(step == 0, chooser(cache_size, places(came)), take)
            return take, lax.dynamic_update_slice(own, mm(take, came).astype(BF), (0, begin))

        state = (jnp.zeros((cache_size, device_count * slot_cap), BF), jnp.zeros_like(row))
        return lax.fori_loop(0, blocks, some_columns, state)[1]

    own, marks = call(
        unpack_kernel,
        None,
        [arrived],
        (of((cache_size, arrived.shape[1]), BF), of((1, LANES), F32)),
        [],
        arrived.shape[1],
    )
    ran_out = jnp.isnan(marks[0, 0]) | jnp.isnan(leg_mark.astype(F32))
    own = lax.cond(ran_out, straight, lambda: own)
    own_part, own_meta = own[:, :wide], own[:, wide:]
    own_turns = turns_of(own_meta[:, 1].astype(F32))
    other = swap(own_part)
    lower, upper = pick(own_part, other), pick(other, own_part)
    own_tokens = jnp.concatenate([lower[:, :half_width], upper[:, :half_width]], axis=1)
    own_context0 = jnp.concatenate([lower[:, half_width:], upper[:, half_width:]], axis=1)
    own_kv0 = own_by_pieces(place, own_tokens, rows0, own_turns, pieces)
    _, own_hidden0 = finish(own_part[:, :half_width], own_context0, out0, out_bias0)
    own_kv1 = project_whole(own_hidden0, rows1, own_turns, None, gathered)

    kept_kv = pick(own_kv0, own_kv1)
    got_kv = swap(pick(own_kv1, own_kv0))
    low_kv, high_kv = pick(kept_kv, got_kv), pick(got_kv, kept_kv)
    cache = jnp.concatenate(
        [low_kv[:, :part], high_kv[:, :part], low_kv[:, part:], high_kv[:, part:]], axis=1
    )
    hidden = pick(hidden0, hidden1).reshape(1, micro_count, row_count, width)
    return hidden, cache[None]


def solution(mesh):
    torus = Mesh(mesh.devices.reshape(2, 4, 4, 8), ("pipe", *DP))
    placed = (
        P(None, DP, None),
        P(None, DP),
        P(None, DP),
        P("pipe", None),
        P("pipe", None),
        P("pipe", DP, None),
        P("pipe", None),
        P("pipe", DP, None),
        P("pipe", None),
    )
    return jax.shard_map(
        shards,
        mesh=torus,
        in_specs=placed,
        out_specs=(P("pipe", None, DP, None), P("pipe", DP, None)),
        check_vma=False,
    )
```

```python
import functools

import jax
import jax.numpy as jnp
from jax import lax
from jax.experimental import pallas as pl
from jax.experimental.pallas import tpu as pltpu
from jax.sharding import Mesh
from jax.sharding import PartitionSpec as P

HDIM = 256
ROT = 64
HALF = ROT // 2
EPS = 1e-05
META = 128
LANES = 128
TILE = 256
BF = jnp.bfloat16
F32 = jnp.float32
DP = ("x", "y", "z")
PLANE = ("x", "y")
CAP_Z = 48
CAP_P = 32


def swap(value):
    return lax.ppermute(value, "pipe", [(0, 1), (1, 0)])


def mm(a, b):
    return jnp.dot(a, b, preferred_element_type=F32)


def chooser(count, places):
    return (jnp.arange(count, dtype=jnp.int32)[:, None] == places[None, :]).astype(BF)


def slots_of(dest, valid, count, cap):
    rows = dest.shape[0]
    hits = ((dest[:, None] == jnp.arange(count, dtype=jnp.int32)[None, :]) & valid[:, None]).astype(BF)
    number = jnp.arange(rows, dtype=jnp.int32)
    before = mm((number[None, :] < number[:, None]).astype(BF), hits)
    rank = jnp.sum(before * hits.astype(F32), axis=1).astype(jnp.int32)
    fits = valid & (rank < cap)
    return jnp.where(fits, dest * cap + rank, -1), jnp.any(valid & (rank >= cap))


def across(filled, axes, cap):
    cols = filled.shape[1]
    arrived = lax.all_to_all(
        filled.reshape(-1, cap, cols), axes, split_axis=0, concat_axis=0, tiled=True
    )
    return arrived.reshape(-1, cols)


def turns_of(positions):
    lane = jnp.arange(LANES)
    inverse = 10000.0 ** (-2.0 * (lane % HALF).astype(F32) / ROT)
    angles = positions[:, None] * inverse[None, :]
    cosine, sine = jnp.cos(angles), jnp.sin(angles)
    rotated, first = (lane < ROT)[None, :], (lane < HALF)[None, :]
    return jnp.stack(
        [
            jnp.where(rotated, cosine, 1.0),
            jnp.where(first, -sine, 0.0),
            jnp.where(rotated & ~first, sine, 0.0),
        ]
    )


def layer_norm(layer_in, gain_row, shift_row):
    data = layer_in.astype(F32)
    centre = jnp.mean(data, axis=-1, keepdims=True)
    centred = data - centre
    variance = jnp.mean(centred * centred, axis=-1, keepdims=True)
    return (centred * lax.rsqrt(variance + EPS) * gain_row + shift_row).astype(BF)


def rotary(cols, turns):
    parts = []
    for first in range(0, cols.shape[1], HDIM):
        head = cols[:, first : first + LANES]
        parts.append(
            head * turns[0]
            + pltpu.roll(head, LANES - HALF, 1) * turns[1]
            + pltpu.roll(head, HALF, 1) * turns[2]
        )
        parts.append(cols[:, first + LANES : first + HDIM])
    return jnp.concatenate(parts, axis=1).astype(BF)


def attend(queries, key_rows, value_rows, allowed):
    parts = []
    for first in range(0, queries.shape[1], HDIM):
        one = slice(first, first + HDIM)
        scores = lax.dot_general(
            queries[:, one], key_rows[:, one], (((1,), (1,)), ((), ())), preferred_element_type=F32
        ) * HDIM ** (-0.5)
        scores = jnp.where(allowed > 0, scores, -1e30)
        exp_scores = jnp.exp(scores - jnp.max(scores, axis=-1, keepdims=True))
        probs = (exp_scores / jnp.sum(exp_scores, axis=-1, keepdims=True)).astype(BF)
        parts.append(mm(probs, value_rows[:, one]).astype(BF))
    return jnp.concatenate(parts, axis=1)


def conclude(projected, turns, allowed_ref, out_ref):
    turns = [turns[k] for k in range(3)]
    if allowed_ref is None:
        half = projected.shape[1] // 2
        out_ref[:, :half] = rotary(projected[:, :half], turns)
        out_ref[:, half:] = projected[:, half:].astype(BF)
    else:
        third = projected.shape[1] // 3
        queries = rotary(projected[:, :third], turns)
        key_rows = rotary(projected[:, third : 2 * third], turns)
        value_rows = projected[:, 2 * third :].astype(BF)
        out_ref[...] = attend(queries, key_rows, value_rows, allowed_ref[...])


NEAR = ((0, 0, 4), (1, 0, 4), (3, 0, 4))
FAR = ((2, 0, 2), (2, 2, 2))


def cut(whole, normed):
    for k in range(normed.shape[0]):
        normed[k] = whole[:, k * LANES : (k + 1) * LANES]


def add_pieces(place, normed, parts, pieces, base, total, skipped):
    def left_hand(which, k, first, count):
        blocks = []
        for j in range(first, first + count):
            x_step, y_step = (k, j) if which == 0 else (j, k)
            x = lax.rem(place[0] + x_step, 4)
            y = lax.rem(place[1] + y_step, 4)
            blocks.append(normed[x * 4 + y])
        return jnp.concatenate(blocks, axis=1)

    def tile(which, number):
        column = pl.ds(pl.multiple_of(number * TILE, TILE), TILE)
        of_ring = pieces[len(parts) * which : len(parts) * (which + 1)]
        target = pl.ds(pl.multiple_of((3 * which + number) * TILE - skipped, TILE), TILE)
        result = jnp.broadcast_to(base[:, target], (total.shape[0], TILE))
        for part, piece in zip(parts, of_ring):
            result = result + mm(left_hand(which, *part), piece[:, column])
        total[:, target] = result

    for which in range(2):
        pl.loop(0 if which else skipped // TILE, 3)(functools.partial(tile, which))


def near_kernel(place, layer_in, gain, shift, bias, *rest):
    pieces, total, normed = rest[:-2], rest[-2], rest[-1]
    cut(layer_norm(layer_in[...], gain[...], shift[...]), normed)
    add_pieces(place, normed, NEAR, pieces, bias, total, 0)


def far_kernel(place, normed, near, turns, allowed, *rest):
    pieces, out_ref, total = rest[:-2], rest[-2], rest[-1]
    add_pieces(place, normed, FAR, pieces, near, total, 0)
    conclude(total[...], turns, allowed, out_ref)


def own_kernel(place, layer_in, gain, shift, bias, turns, *rest):
    pieces, out_ref, normed, total = rest[:-3], rest[-3], rest[-2], rest[-1]
    cut(layer_norm(layer_in[...], gain[...], shift[...]), normed)
    add_pieces(place, normed, NEAR + FAR, pieces, bias, total, 2 * TILE)
    conclude(total[...], turns, None, out_ref)


def unpack_kernel(came, own, marks):
    blocks = came.shape[1] // LANES
    last = came[:, (blocks - 1) * LANES :].astype(F32)
    lane = lax.broadcasted_iota(jnp.int32, last.shape, 1)
    named = jnp.sum(jnp.where(lane == 0, last, 0.0), axis=1, keepdims=True)
    take = (lane.astype(F32) + 1.0 == named).astype(BF)
    for first in range(0, blocks * LANES, 4 * LANES):
        part = came[:, first : min(first + 4 * LANES, blocks * LANES)]
        own[:, first : first + part.shape[1]] = lax.dot_general(
            take, part, (((0,), (0,)), ((), ())), preferred_element_type=F32
        ).astype(BF)
    marks[...] = jnp.sum(came[:, 8 * LANES : 9 * LANES].astype(F32), axis=0, keepdims=True)


def whole_kernel(with_context, layer_in, gain, shift, bias, turns, *rest):
    allowed, rest = (rest[0], rest[1:]) if with_context else (None, rest)
    weights, out_ref, normed, total = rest[:-3], rest[-3], rest[-2], rest[-1]
    step = pl.program_id(0)
    depth = weights[0].shape[0]

    @pl.when(step == 0)
    def _():
        whole = layer_norm(layer_in[...], gain[...], shift[...])
        for k in range(normed.shape[0]):
            normed[k] = whole[:, k * depth : (k + 1) * depth]
        total[...] = jnp.broadcast_to(bias[...], total.shape)

    part = normed[step]
    first = 0
    for one in weights:
        width = one.shape[1]
        total[:, first : first + width] += mm(part, one[...])
        first += width

    @pl.when(step == pl.num_programs(0) - 1)
    def _():
        conclude(total[...], turns, allowed, out_ref)


def cost(rows, width, cols):
    return pl.CostEstimate(flops=rows * cols, bytes_accessed=rows * cols, transcendentals=0)


def call(kernel, place, operands, out_shape, scratch, columns):
    rows = 128
    in_specs = [pl.BlockSpec(memory_space=pltpu.VMEM)] * len(operands)
    if place is not None:
        operands = [place, *operands]
        in_specs = [pl.BlockSpec(memory_space=pltpu.SMEM), *in_specs]
    return pl.pallas_call(
        kernel,
        out_shape=out_shape,
        in_specs=in_specs,
        out_specs=jax.tree.map(lambda one: pl.BlockSpec(memory_space=pltpu.VMEM), out_shape),
        scratch_shapes=[pltpu.VMEM(*one) for one in scratch],
        cost_estimate=cost(rows, rows, columns),
        compiler_params=pltpu.CompilerParams(vmem_limit_bytes=24 << 20),
    )(*operands)


def of(shape, dtype):
    return jax.ShapeDtypeStruct(shape, dtype)


def context_by_pieces(place, layer_in, vectors, turns, allowed, pieces):
    rows = layer_in.shape[0]
    columns = vectors[2].shape[1]
    sums, blocks = of((rows, columns), F32), of((16, rows, LANES), BF)
    near = [*pieces[:3], *pieces[5:8]]
    far = [*pieces[3:5], *pieces[8:]]
    total, normed = call(near_kernel, place, [layer_in, *vectors, *near], (sums, blocks), [], columns)
    return call(
        far_kernel,
        place,
        [normed, total, turns, allowed, *far],
        of((rows, 512), BF),
        [((rows, columns), F32)],
        columns,
    )


def own_by_pieces(place, layer_in, vectors, turns, pieces):
    rows = layer_in.shape[0]
    gain, shift, bias = vectors
    bias = bias[:, 512:]
    return call(
        own_kernel,
        place,
        [layer_in, gain, shift, bias, turns, *pieces],
        of((rows, 1024), BF),
        [((16, rows, LANES), BF), ((rows, 1024), F32)],
        1024,
    )


def project_whole(layer_in, vectors, turns, allowed, gathered):
    rows, width = layer_in.shape
    gain, shift, bias = vectors
    with_context = allowed is not None
    out_cols = 512 if with_context else 1024
    if not with_context:
        bias = bias[:, 512:]
    operands = [layer_in, gain, shift, bias, turns, *((allowed,) if with_context else ())]
    depth = 512
    columns = (0, 1, 2) if with_context else (1, 2)
    return pl.pallas_call(
        functools.partial(whole_kernel, with_context),
        grid=(width // depth,),
        out_shape=jax.ShapeDtypeStruct((rows, out_cols), BF),
        in_specs=[
            pl.BlockSpec(one.shape, lambda k, rank=one.ndim: (0,) * rank) for one in operands
        ]
        + [pl.BlockSpec((depth, 512), lambda k, col=col: (k, col)) for col in columns],
        out_specs=pl.BlockSpec((rows, out_cols), lambda k: (0, 0)),
        scratch_shapes=[
            pltpu.VMEM((width // depth, rows, depth), BF),
            pltpu.VMEM((rows, bias.shape[1]), F32),
        ],
        cost_estimate=cost(rows, width, bias.shape[1]),
        compiler_params=pltpu.CompilerParams(vmem_limit_bytes=24 << 20),
    )(*operands, *[pltpu.with_memory_space_constraint(gathered, pltpu.HBM)] * len(columns))


def shifted(value, axis, by):
    size = lax.axis_size(axis)
    return lax.ppermute(value, axis, [(one, (one + by) % size) for one in range(size)])


def rings(blocks, axes, halves, later=()):
    size = lax.axis_size(axes[0])
    found = [{0: [block]} for block in blocks]
    ups = downs = list(blocks)
    for step in range(1, size // 2):
        ups = [shifted(up, axis, 1) for up, axis in zip(ups, axes)]
        downs = [shifted(down, axis, -1) for down, axis in zip(downs, axes)]
        ups, downs, later = lax.optimization_barrier((ups, downs, later))
        for one, up, down in zip(found, ups, downs):
            one[size - step], one[step] = [up], [down]
    for one, up, down, axis in zip(found, ups, downs, axes):
        rows = up.shape[0] // 2
        if halves:
            one[size // 2] = [shifted(up[:rows], axis, 1), shifted(down[rows:], axis, -1)]
        else:
            one[size // 2] = [shifted(up, axis, 1)]
    return [[one[k] for k in range(size)] for one in found], later


def column_of(shard):
    size, index = lax.axis_size("z"), lax.axis_index("z")
    block, step = shard[None], size // 2
    while step:
        got = lax.ppermute(block, "z", [(one, one ^ step) for one in range(size)])
        upper = (index // step) % 2 == 1
        both = [jnp.where(upper, got, block), jnp.where(upper, block, got)]
        block = jnp.stack(both, axis=1).reshape(-1, *shard.shape)
        step //= 2
    return block.reshape(-1, shard.shape[1])


def pieces_of(ring, later):
    half = ring.shape[1] // 2
    pair, later = rings([ring[:, :half], ring[:, half:]], ["y", "x"], False, later)
    pair = [jnp.concatenate([one[0] for one in each], axis=0) for each in pair]
    pair = lax.optimization_barrier(pair)
    order = []
    for each in rings(pair, ["x", "y"], True)[0]:
        order += [*each[0], *each[1], *each[3], *each[2]]
    return order, later


def shards(
    tokens, seg_ids, cache_row, ln_gain, ln_bias, qkv_weight, qkv_bias, out_weight, out_bias
):
    micro_count, row_count, width = tokens.shape
    device_count = lax.axis_size(DP)
    first_core = lax.axis_index("pipe") == 0
    cache_size = micro_count * row_count
    slot_cap = 2 * micro_count * ((row_count + device_count - 1) // device_count)
    head_width = qkv_weight.shape[2] // 3
    part = head_width // 2
    half_width = width // 2

    def pick(a, b):
        return jnp.where(first_core, a, b)

    def joined(piece):
        other = swap(piece)
        return jnp.concatenate([pick(piece, other), pick(other, piece)], axis=1)

    def packed(which):
        cuts = [
            qkv_weight[0][:, kind * head_width + which * part : kind * head_width + (which + 1) * part]
            for kind in range(3)
        ]
        begin = which * half_width
        out_cut = jnp.concatenate(
            [out_weight[0][:, begin : begin + part], out_weight[0][:, begin + part : begin + 2 * part]],
            axis=0,
        )
        return jnp.concatenate([*cuts, out_cut], axis=1)

    low, high = packed(0), packed(1)
    kept = pick(low, high)
    got = swap(pick(high, low))
    shard0, shard1 = pick(kept, got), pick(got, kept)
    bulk = jnp.concatenate([shard1, shard0[:, 3 * part :]], axis=1)
    gathered = lax.all_gather(bulk, DP, axis=0, tiled=True)
    pieces, (tokens, seg_ids, cache_row, ln_gain) = pieces_of(
        column_of(shard0[:, : 3 * part]), (tokens, seg_ids, cache_row, ln_gain)
    )

    vectors = jnp.concatenate([ln_gain[0], ln_bias[0], qkv_bias[0], out_bias[0]])
    vectors_got = swap(vectors)

    def vectors_of(layer):
        vec = pick(vectors, vectors_got) if layer == 0 else pick(vectors_got, vectors)
        rest = vec[2 * width :]
        bias = [
            pick(
                rest[kind * head_width : kind * head_width + part],
                rest[kind * head_width + part : (kind + 1) * head_width],
            )
            for kind in range(3)
        ]
        out_b = rest[3 * head_width :]
        rows = (vec[None, :width], vec[None, width : 2 * width], jnp.concatenate(bias)[None, :])
        return rows, pick(out_b[:half_width], out_b[half_width:])

    (rows0, out_bias0), (rows1, out_bias1) = vectors_of(0), vectors_of(1)

    flat = tokens.reshape(cache_size, width)
    seg = seg_ids.reshape(cache_size)
    rows = cache_row.reshape(cache_size)
    order = jnp.arange(cache_size, dtype=jnp.int32)
    micro = order // row_count
    same_micro = micro[:, None] == micro[None, :]
    positions = (order % row_count) - jnp.sum(
        (same_micro & (seg[None, :] < seg[:, None])).astype(jnp.int32), axis=1
    )
    earlier = order[None, :] <= order[:, None]
    allowed = (same_micro & earlier & (seg[:, None] == seg[None, :])).astype(F32)
    owners = rows // cache_size
    rank = jnp.sum(
        (same_micro & earlier & (owners[:, None] == owners[None, :])).astype(jnp.int32), axis=1
    ) - 1
    slot = owners * slot_cap + micro * (slot_cap // micro_count) + rank
    depth = lax.axis_size("z")
    lane = jnp.arange(META, dtype=jnp.int32)[None, :]
    meta = jnp.where(
        lane == 0,
        (rows % cache_size + 1)[:, None],
        jnp.where(lane == 1, positions[:, None], jnp.where(lane == 2, (owners // depth)[:, None], 0)),
    ).astype(BF)
    half_tokens = pick(flat[:, :half_width], flat[:, half_width:])
    payload = jnp.concatenate([half_tokens, meta], axis=1)
    flag_at = half_width + 3

    def flagged(filled, flag, at):
        mark = (jnp.arange(filled.shape[1]) == at).astype(BF)[None, :]
        return filled + flag.astype(BF) * mark

    slot_z, out_z = slots_of(owners % depth, rows >= 0, depth, CAP_Z)
    send_z = chooser(depth * CAP_Z, slot_z)
    filled = flagged(mm(send_z, payload).astype(BF), out_z, flag_at)
    place = jnp.stack([lax.axis_index("x"), lax.axis_index("y")]).astype(jnp.int32)
    turns = turns_of(positions.astype(F32))
    middle = across(filled, "z", CAP_Z)
    slot_p, out_p = slots_of(
        middle[:, half_width + 2].astype(jnp.int32),
        middle[:, half_width] > 0,
        device_count // depth,
        CAP_P,
    )
    slots_p = device_count // depth * CAP_P
    send_p = chooser(slots_p, slot_p)
    ran_out = out_p | jnp.any(middle[:, flag_at] > 0)

    context0 = context_by_pieces(place, flat, rows0, turns, allowed, pieces)
    filled = jnp.where(ran_out, jnp.nan, mm(send_z, context0)).astype(BF)
    middle0 = across(filled, "z", CAP_Z)
    leg = jnp.concatenate([middle[:, :half_width], middle0, middle[:, half_width:]], axis=1)
    leg = mm(send_p, leg).astype(BF)
    wide = half_width + part
    arrived = across(leg, PLANE, CAP_P)
    gathered, leg_mark, rows1, out_bias0, out_bias1 = lax.optimization_barrier(
        (gathered, leg[0, half_width], rows1, out_bias0, out_bias1)
    )

    def finish(half, context, out, out_b):
        done = jnp.concatenate([mm(context, one) for one in out], axis=1)
        done = (half.astype(F32) + done + out_b).astype(BF)
        return done, joined(done)

    def out_of(begin):
        cut = gathered[:, begin : begin + part].reshape(device_count, 2, -1, part)
        return [cut[:, k].reshape(head_width, part) for k in range(2)]

    out0, out1 = out_of(4 * part), out_of(3 * part)
    hidden0_half, hidden0 = finish(half_tokens, joined(context0), out0, out_bias0)
    arrived, hidden0_half = lax.optimization_barrier((arrived, hidden0_half))
    context1 = project_whole(hidden0, rows1, turns, allowed, gathered)
    _, hidden1 = finish(hidden0_half, joined(context1), out1, out_bias1)

    def places(came_meta):
        return came_meta[:, 0].astype(jnp.int32) - 1

    def straight():
        row = jnp.concatenate([half_tokens, context0, meta], axis=1)
        fill = chooser(device_count * slot_cap, slot)
        blocks = row.shape[1] // META

        def some_columns(step, state):
            take, own = state
            begin = (blocks - 1 - step) * META
            part_of = lax.dynamic_slice_in_dim(row, begin, META, 1)
            came = across(mm(fill, part_of).astype(BF), DP, slot_cap)
            take = jnp.where(step == 0, chooser(cache_size, places(came)), take)
            return take, lax.dynamic_update_slice(own, mm(take, came).astype(BF), (0, begin))

        state = (jnp.zeros((cache_size, device_count * slot_cap), BF), jnp.zeros_like(row))
        return lax.fori_loop(0, blocks, some_columns, state)[1]

    own, marks = call(
        unpack_kernel,
        None,
        [arrived],
        (of((cache_size, arrived.shape[1]), BF), of((1, LANES), F32)),
        [],
        arrived.shape[1],
    )
    ran_out = jnp.isnan(marks[0, 0]) | jnp.isnan(leg_mark.astype(F32))
    own = lax.cond(ran_out, straight, lambda: own)
    own_part, own_meta = own[:, :wide], own[:, wide:]
    own_turns = turns_of(own_meta[:, 1].astype(F32))
    other = swap(own_part)
    lower, upper = pick(own_part, other), pick(other, own_part)
    own_tokens = jnp.concatenate([lower[:, :half_width], upper[:, :half_width]], axis=1)
    own_context0 = jnp.concatenate([lower[:, half_width:], upper[:, half_width:]], axis=1)
    own_kv0 = own_by_pieces(place, own_tokens, rows0, own_turns, pieces)
    _, own_hidden0 = finish(own_part[:, :half_width], own_context0, out0, out_bias0)
    own_kv1 = project_whole(own_hidden0, rows1, own_turns, None, gathered)

    kept_kv = pick(own_kv0, own_kv1)
    got_kv = swap(pick(own_kv1, own_kv0))
    low_kv, high_kv = pick(kept_kv, got_kv), pick(got_kv, kept_kv)
    cache = jnp.concatenate(
        [low_kv[:, :part], high_kv[:, :part], low_kv[:, part:], high_kv[:, part:]], axis=1
    )
    hidden = pick(hidden0, hidden1).reshape(1, micro_count, row_count, width)
    return hidden, cache[None]


def solution(mesh):
    torus = Mesh(mesh.devices.reshape(2, 4, 4, 8), ("pipe", *DP))
    placed = (
        P(None, DP, None),
        P(None, DP),
        P(None, DP),
        P("pipe", None),
        P("pipe", None),
        P("pipe", DP, None),
        P("pipe", None),
        P("pipe", DP, None),
        P("pipe", None),
    )
    return jax.shard_map(
        shards,
        mesh=torus,
        in_specs=placed,
        out_specs=(P("pipe", None, DP, None), P("pipe", DP, None)),
        check_vma=False,
    )
```

```python
import functools

import jax
import jax.numpy as jnp
from jax import lax
from jax.experimental import pallas as pl
from jax.experimental.pallas import tpu as pltpu
from jax.sharding import Mesh
from jax.sharding import PartitionSpec as P

HDIM = 256
ROT = 64
HALF = ROT // 2
EPS = 1e-05
META = 128
LANES = 128
TILE = 256
BF = jnp.bfloat16
F32 = jnp.float32
DP = ("x", "y", "z")
PLANE = ("x", "y")
CAP_Z = 48
CAP_P = 32


def swap(value):
    return lax.ppermute(value, "pipe", [(0, 1), (1, 0)])


def mm(a, b):
    return jnp.dot(a, b, preferred_element_type=F32)


def chooser(count, places):
    return (jnp.arange(count, dtype=jnp.int32)[:, None] == places[None, :]).astype(BF)


def slots_of(dest, valid, count, cap):
    rows = dest.shape[0]
    hits = ((dest[:, None] == jnp.arange(count, dtype=jnp.int32)[None, :]) & valid[:, None]).astype(BF)
    number = jnp.arange(rows, dtype=jnp.int32)
    before = mm((number[None, :] < number[:, None]).astype(BF), hits)
    rank = jnp.sum(before * hits.astype(F32), axis=1).astype(jnp.int32)
    fits = valid & (rank < cap)
    return jnp.where(fits, dest * cap + rank, -1), jnp.any(valid & (rank >= cap))


def across(filled, axes, cap):
    cols = filled.shape[1]
    arrived = lax.all_to_all(
        filled.reshape(-1, cap, cols), axes, split_axis=0, concat_axis=0, tiled=True
    )
    return arrived.reshape(-1, cols)


def turns_of(positions):
    lane = jnp.arange(LANES)
    inverse = 10000.0 ** (-2.0 * (lane % HALF).astype(F32) / ROT)
    angles = positions[:, None] * inverse[None, :]
    cosine, sine = jnp.cos(angles), jnp.sin(angles)
    rotated, first = (lane < ROT)[None, :], (lane < HALF)[None, :]
    return jnp.stack(
        [
            jnp.where(rotated, cosine, 1.0),
            jnp.where(first, -sine, 0.0),
            jnp.where(rotated & ~first, sine, 0.0),
        ]
    )


def layer_norm(layer_in, gain_row, shift_row):
    data = layer_in.astype(F32)
    centre = jnp.mean(data, axis=-1, keepdims=True)
    centred = data - centre
    variance = jnp.mean(centred * centred, axis=-1, keepdims=True)
    return (centred * lax.rsqrt(variance + EPS) * gain_row + shift_row).astype(BF)


def rotary(cols, turns):
    parts = []
    for first in range(0, cols.shape[1], HDIM):
        head = cols[:, first : first + LANES]
        parts.append(
            head * turns[0]
            + pltpu.roll(head, LANES - HALF, 1) * turns[1]
            + pltpu.roll(head, HALF, 1) * turns[2]
        )
        parts.append(cols[:, first + LANES : first + HDIM])
    return jnp.concatenate(parts, axis=1).astype(BF)


def attend(queries, key_rows, value_rows, allowed):
    parts = []
    for first in range(0, queries.shape[1], HDIM):
        one = slice(first, first + HDIM)
        scores = lax.dot_general(
            queries[:, one], key_rows[:, one], (((1,), (1,)), ((), ())), preferred_element_type=F32
        ) * HDIM ** (-0.5)
        scores = jnp.where(allowed > 0, scores, -1e30)
        exp_scores = jnp.exp(scores - jnp.max(scores, axis=-1, keepdims=True))
        probs = (exp_scores / jnp.sum(exp_scores, axis=-1, keepdims=True)).astype(BF)
        parts.append(mm(probs, value_rows[:, one]).astype(BF))
    return jnp.concatenate(parts, axis=1)


def conclude(projected, turns, allowed_ref, out_ref):
    turns = [turns[k] for k in range(3)]
    if allowed_ref is None:
        half = projected.shape[1] // 2
        out_ref[:, :half] = rotary(projected[:, :half], turns)
        out_ref[:, half:] = projected[:, half:].astype(BF)
    else:
        third = projected.shape[1] // 3
        queries = rotary(projected[:, :third], turns)
        key_rows = rotary(projected[:, third : 2 * third], turns)
        value_rows = projected[:, 2 * third :].astype(BF)
        out_ref[...] = attend(queries, key_rows, value_rows, allowed_ref[...])


NEAR = ((0, 0, 4), (1, 0, 4), (3, 0, 4))
FAR = ((2, 0, 2), (2, 2, 2))


def cut(whole, normed):
    for k in range(normed.shape[0]):
        normed[k] = whole[:, k * LANES : (k + 1) * LANES]


def add_pieces(place, normed, parts, pieces, base, total, skipped):
    def left_hand(which, k, first, count):
        blocks = []
        for j in range(first, first + count):
            x_step, y_step = (k, j) if which == 0 else (j, k)
            x = lax.rem(place[0] + x_step, 4)
            y = lax.rem(place[1] + y_step, 4)
            blocks.append(normed[x * 4 + y])
        return jnp.concatenate(blocks, axis=1)

    def tile(which, number):
        column = pl.ds(pl.multiple_of(number * TILE, TILE), TILE)
        of_ring = pieces[len(parts) * which : len(parts) * (which + 1)]
        target = pl.ds(pl.multiple_of((3 * which + number) * TILE - skipped, TILE), TILE)
        result = jnp.broadcast_to(base[:, target], (total.shape[0], TILE))
        for part, piece in zip(parts, of_ring):
            result = result + mm(left_hand(which, *part), piece[:, column])
        total[:, target] = result

    for which in range(2):
        pl.loop(0 if which else skipped // TILE, 3)(functools.partial(tile, which))


def near_kernel(place, layer_in, gain, shift, bias, *rest):
    pieces, total, normed = rest[:-2], rest[-2], rest[-1]
    cut(layer_norm(layer_in[...], gain[...], shift[...]), normed)
    add_pieces(place, normed, NEAR, pieces, bias, total, 0)


def far_kernel(place, normed, near, turns, allowed, *rest):
    pieces, out_ref, total = rest[:-2], rest[-2], rest[-1]
    add_pieces(place, normed, FAR, pieces, near, total, 0)
    conclude(total[...], turns, allowed, out_ref)


def own_kernel(place, layer_in, gain, shift, bias, turns, *rest):
    pieces, out_ref, normed, total = rest[:-3], rest[-3], rest[-2], rest[-1]
    cut(layer_norm(layer_in[...], gain[...], shift[...]), normed)
    add_pieces(place, normed, NEAR + FAR, pieces, bias, total, 2 * TILE)
    conclude(total[...], turns, None, out_ref)


def unpack_kernel(came, own, marks):
    blocks = came.shape[1] // LANES
    last = came[:, (blocks - 1) * LANES :].astype(F32)
    lane = lax.broadcasted_iota(jnp.int32, last.shape, 1)
    named = jnp.sum(jnp.where(lane == 0, last, 0.0), axis=1, keepdims=True)
    take = (lane.astype(F32) + 1.0 == named).astype(BF)
    for first in range(0, blocks * LANES, 4 * LANES):
        part = came[:, first : min(first + 4 * LANES, blocks * LANES)]
        own[:, first : first + part.shape[1]] = lax.dot_general(
            take, part, (((0,), (0,)), ((), ())), preferred_element_type=F32
        ).astype(BF)
    marks[...] = jnp.sum(came[:, 8 * LANES : 9 * LANES].astype(F32), axis=0, keepdims=True)


def whole_kernel(with_context, layer_in, gain, shift, bias, turns, *rest):
    allowed, rest = (rest[0], rest[1:]) if with_context else (None, rest)
    weights, out_ref, normed, total = rest[:-3], rest[-3], rest[-2], rest[-1]
    step = pl.program_id(0)
    depth = weights[0].shape[0]

    @pl.when(step == 0)
    def _():
        whole = layer_norm(layer_in[...], gain[...], shift[...])
        for k in range(normed.shape[0]):
            normed[k] = whole[:, k * depth : (k + 1) * depth]
        total[...] = jnp.broadcast_to(bias[...], total.shape)

    part = normed[step]
    first = 0
    for one in weights:
        width = one.shape[1]
        total[:, first : first + width] += mm(part, one[...])
        first += width

    @pl.when(step == pl.num_programs(0) - 1)
    def _():
        conclude(total[...], turns, allowed, out_ref)


def slots_kernel(cap, meta, choice, flag):
    info = meta[...].astype(F32)
    lane = lax.broadcasted_iota(jnp.int32, info.shape, 1)

    def column(k):
        return jnp.sum(jnp.where(lane == k, info, 0.0), axis=1, keepdims=True)

    valid = jnp.where(column(0) > 0.0, 1.0, 0.0)
    dest = column(2)
    hits = jnp.where(lane.astype(F32) == dest, 1.0, 0.0) * valid
    square = (info.shape[0], info.shape[0])
    row = lax.broadcasted_iota(jnp.int32, square, 0)
    earlier = jnp.where(lax.broadcasted_iota(jnp.int32, square, 1) < row, 1.0, 0.0)
    before = mm(earlier.astype(BF), hits.astype(BF))
    rank = jnp.sum(before * hits, axis=1, keepdims=True)
    slot = jnp.where(rank < cap, dest * cap + rank, -1.0) * valid + (valid - 1.0)
    place = lax.broadcasted_iota(jnp.int32, choice.shape, 1).astype(F32)
    choice[...] = jnp.where(place == slot, 1.0, 0.0).astype(BF)
    over = jnp.where(rank < cap, 0.0, 1.0) * valid + column(3)
    flag[...] = jnp.broadcast_to(jnp.sum(over, axis=0, keepdims=True), flag.shape)


def cost(rows, width, cols):
    return pl.CostEstimate(flops=rows * cols, bytes_accessed=rows * cols, transcendentals=0)


def call(kernel, place, operands, out_shape, scratch, columns):
    rows = 128
    in_specs = [pl.BlockSpec(memory_space=pltpu.VMEM)] * len(operands)
    if place is not None:
        operands = [place, *operands]
        in_specs = [pl.BlockSpec(memory_space=pltpu.SMEM), *in_specs]
    return pl.pallas_call(
        kernel,
        out_shape=out_shape,
        in_specs=in_specs,
        out_specs=jax.tree.map(lambda one: pl.BlockSpec(memory_space=pltpu.VMEM), out_shape),
        scratch_shapes=[pltpu.VMEM(*one) for one in scratch],
        cost_estimate=cost(rows, rows, columns),
        compiler_params=pltpu.CompilerParams(vmem_limit_bytes=24 << 20),
    )(*operands)


def of(shape, dtype):
    return jax.ShapeDtypeStruct(shape, dtype)


def context_by_pieces(place, layer_in, vectors, turns, allowed, pieces):
    rows = layer_in.shape[0]
    columns = vectors[2].shape[1]
    sums, blocks = of((rows, columns), F32), of((16, rows, LANES), BF)
    near = [*pieces[:3], *pieces[5:8]]
    far = [*pieces[3:5], *pieces[8:]]
    total, normed = call(near_kernel, place, [layer_in, *vectors, *near], (sums, blocks), [], columns)
    return call(
        far_kernel,
        place,
        [normed, total, turns, allowed, *far],
        of((rows, 512), BF),
        [((rows, columns), F32)],
        columns,
    )


def own_by_pieces(place, layer_in, vectors, turns, pieces):
    rows = layer_in.shape[0]
    gain, shift, bias = vectors
    bias = bias[:, 512:]
    return call(
        own_kernel,
        place,
        [layer_in, gain, shift, bias, turns, *pieces],
        of((rows, 1024), BF),
        [((16, rows, LANES), BF), ((rows, 1024), F32)],
        1024,
    )


def project_whole(layer_in, vectors, turns, allowed, gathered):
    rows, width = layer_in.shape
    gain, shift, bias = vectors
    with_context = allowed is not None
    out_cols = 512 if with_context else 1024
    if not with_context:
        bias = bias[:, 512:]
    operands = [layer_in, gain, shift, bias, turns, *((allowed,) if with_context else ())]
    depth = 512
    columns = (0, 1, 2) if with_context else (1, 2)
    return pl.pallas_call(
        functools.partial(whole_kernel, with_context),
        grid=(width // depth,),
        out_shape=jax.ShapeDtypeStruct((rows, out_cols), BF),
        in_specs=[
            pl.BlockSpec(one.shape, lambda k, rank=one.ndim: (0,) * rank) for one in operands
        ]
        + [pl.BlockSpec((depth, 512), lambda k, col=col: (k, col)) for col in columns],
        out_specs=pl.BlockSpec((rows, out_cols), lambda k: (0, 0)),
        scratch_shapes=[
            pltpu.VMEM((width // depth, rows, depth), BF),
            pltpu.VMEM((rows, bias.shape[1]), F32),
        ],
        cost_estimate=cost(rows, width, bias.shape[1]),
        compiler_params=pltpu.CompilerParams(vmem_limit_bytes=24 << 20),
    )(*operands, *[pltpu.with_memory_space_constraint(gathered, pltpu.HBM)] * len(columns))


def shifted(value, axis, by):
    size = lax.axis_size(axis)
    return lax.ppermute(value, axis, [(one, (one + by) % size) for one in range(size)])


def rings(blocks, axes, halves, later=()):
    size = lax.axis_size(axes[0])
    found = [{0: [block]} for block in blocks]
    ups = downs = list(blocks)
    for step in range(1, size // 2):
        ups = [shifted(up, axis, 1) for up, axis in zip(ups, axes)]
        downs = [shifted(down, axis, -1) for down, axis in zip(downs, axes)]
        ups, downs, later = lax.optimization_barrier((ups, downs, later))
        for one, up, down in zip(found, ups, downs):
            one[size - step], one[step] = [up], [down]
    for one, up, down, axis in zip(found, ups, downs, axes):
        rows = up.shape[0] // 2
        if halves:
            one[size // 2] = [shifted(up[:rows], axis, 1), shifted(down[rows:], axis, -1)]
        else:
            one[size // 2] = [shifted(up, axis, 1)]
    return [[one[k] for k in range(size)] for one in found], later


def column_of(shard):
    size, index = lax.axis_size("z"), lax.axis_index("z")
    block, step = shard[None], size // 2
    while step:
        got = lax.ppermute(block, "z", [(one, one ^ step) for one in range(size)])
        upper = (index // step) % 2 == 1
        both = [jnp.where(upper, got, block), jnp.where(upper, block, got)]
        block = jnp.stack(both, axis=1).reshape(-1, *shard.shape)
        step //= 2
    return block.reshape(-1, shard.shape[1])


def pieces_of(ring, later):
    half = ring.shape[1] // 2
    pair, later = rings([ring[:, :half], ring[:, half:]], ["y", "x"], False, later)
    pair = [jnp.concatenate([one[0] for one in each], axis=0) for each in pair]
    pair = lax.optimization_barrier(pair)
    order = []
    for each in rings(pair, ["x", "y"], True)[0]:
        order += [*each[0], *each[1], *each[3], *each[2]]
    return order, later


def shards(
    tokens, seg_ids, cache_row, ln_gain, ln_bias, qkv_weight, qkv_bias, out_weight, out_bias
):
    micro_count, row_count, width = tokens.shape
    device_count = lax.axis_size(DP)
    first_core = lax.axis_index("pipe") == 0
    cache_size = micro_count * row_count
    slot_cap = 2 * micro_count * ((row_count + device_count - 1) // device_count)
    head_width = qkv_weight.shape[2] // 3
    part = head_width // 2
    half_width = width // 2

    def pick(a, b):
        return jnp.where(first_core, a, b)

    def joined(piece):
        other = swap(piece)
        return jnp.concatenate([pick(piece, other), pick(other, piece)], axis=1)

    def packed(which):
        cuts = [
            qkv_weight[0][:, kind * head_width + which * part : kind * head_width + (which + 1) * part]
            for kind in range(3)
        ]
        begin = which * half_width
        out_cut = jnp.concatenate(
            [out_weight[0][:, begin : begin + part], out_weight[0][:, begin + part : begin + 2 * part]],
            axis=0,
        )
        return jnp.concatenate([*cuts, out_cut], axis=1)

    low, high = packed(0), packed(1)
    kept = pick(low, high)
    got = swap(pick(high, low))
    shard0, shard1 = pick(kept, got), pick(got, kept)
    bulk = jnp.concatenate([shard1, shard0[:, 3 * part :]], axis=1)
    gathered = lax.all_gather(bulk, DP, axis=0, tiled=True)
    pieces, (tokens, seg_ids, cache_row, ln_gain) = pieces_of(
        column_of(shard0[:, : 3 * part]), (tokens, seg_ids, cache_row, ln_gain)
    )

    vectors = jnp.concatenate([ln_gain[0], ln_bias[0], qkv_bias[0], out_bias[0]])
    vectors_got = swap(vectors)

    def vectors_of(layer):
        vec = pick(vectors, vectors_got) if layer == 0 else pick(vectors_got, vectors)
        rest = vec[2 * width :]
        bias = [
            pick(
                rest[kind * head_width : kind * head_width + part],
                rest[kind * head_width + part : (kind + 1) * head_width],
            )
            for kind in range(3)
        ]
        out_b = rest[3 * head_width :]
        rows = (vec[None, :width], vec[None, width : 2 * width], jnp.concatenate(bias)[None, :])
        return rows, pick(out_b[:half_width], out_b[half_width:])

    (rows0, out_bias0), (rows1, out_bias1) = vectors_of(0), vectors_of(1)

    flat = tokens.reshape(cache_size, width)
    seg = seg_ids.reshape(cache_size)
    rows = cache_row.reshape(cache_size)
    order = jnp.arange(cache_size, dtype=jnp.int32)
    micro = order // row_count
    same_micro = micro[:, None] == micro[None, :]
    positions = (order % row_count) - jnp.sum(
        (same_micro & (seg[None, :] < seg[:, None])).astype(jnp.int32), axis=1
    )
    earlier = order[None, :] <= order[:, None]
    allowed = (same_micro & earlier & (seg[:, None] == seg[None, :])).astype(F32)
    owners = rows // cache_size
    rank = jnp.sum(
        (same_micro & earlier & (owners[:, None] == owners[None, :])).astype(jnp.int32), axis=1
    ) - 1
    slot = owners * slot_cap + micro * (slot_cap // micro_count) + rank
    depth = lax.axis_size("z")
    lane = jnp.arange(META, dtype=jnp.int32)[None, :]
    meta = jnp.where(
        lane == 0,
        (rows % cache_size + 1)[:, None],
        jnp.where(lane == 1, positions[:, None], jnp.where(lane == 2, (owners // depth)[:, None], 0)),
    ).astype(BF)
    half_tokens = pick(flat[:, :half_width], flat[:, half_width:])
    payload = jnp.concatenate([half_tokens, meta], axis=1)
    flag_at = half_width + 3

    def flagged(filled, flag, at):
        mark = (jnp.arange(filled.shape[1]) == at).astype(BF)[None, :]
        return filled + flag.astype(BF) * mark

    slot_z, out_z = slots_of(owners % depth, rows >= 0, depth, CAP_Z)
    send_z = chooser(depth * CAP_Z, slot_z)
    filled = flagged(mm(send_z, payload).astype(BF), out_z, flag_at)
    place = jnp.stack([lax.axis_index("x"), lax.axis_index("y")]).astype(jnp.int32)
    turns = turns_of(positions.astype(F32))
    middle = across(filled, "z", CAP_Z)
    slots_p = device_count // depth * CAP_P
    send_p, flags = pl.pallas_call(
        functools.partial(slots_kernel, CAP_P),
        grid=(1,),
        out_shape=(of((middle.shape[0], slots_p), BF), of((1, LANES), F32)),
        in_specs=[pl.BlockSpec((middle.shape[0], META), lambda k: (0, half_width // META))],
        out_specs=(
            pl.BlockSpec((middle.shape[0], slots_p), lambda k: (0, 0)),
            pl.BlockSpec((1, LANES), lambda k: (0, 0)),
        ),
        cost_estimate=cost(128, 128, 128),
    )(middle)
    ran_out = flags[0, 0] > 0

    context0 = context_by_pieces(place, flat, rows0, turns, allowed, pieces)
    filled = jnp.where(ran_out, jnp.nan, mm(send_z, context0)).astype(BF)
    middle0 = across(filled, "z", CAP_Z)
    leg = jnp.concatenate([middle[:, :half_width], middle0, middle[:, half_width:]], axis=1)
    leg = lax.dot_general(
        send_p, leg, (((0,), (0,)), ((), ())), preferred_element_type=F32
    ).astype(BF)
    wide = half_width + part
    arrived = across(leg, PLANE, CAP_P)
    gathered, leg_mark, rows1, out_bias0, out_bias1 = lax.optimization_barrier(
        (gathered, leg[0, half_width], rows1, out_bias0, out_bias1)
    )

    def finish(half, context, out, out_b):
        done = jnp.concatenate([mm(context, one) for one in out], axis=1)
        done = (half.astype(F32) + done + out_b).astype(BF)
        return done, joined(done)

    def out_of(begin):
        cut = gathered[:, begin : begin + part].reshape(device_count, 2, -1, part)
        return [cut[:, k].reshape(head_width, part) for k in range(2)]

    out0, out1 = out_of(4 * part), out_of(3 * part)
    hidden0_half, hidden0 = finish(half_tokens, joined(context0), out0, out_bias0)
    arrived, hidden0_half = lax.optimization_barrier((arrived, hidden0_half))
    context1 = project_whole(hidden0, rows1, turns, allowed, gathered)
    _, hidden1 = finish(hidden0_half, joined(context1), out1, out_bias1)

    def places(came_meta):
        return came_meta[:, 0].astype(jnp.int32) - 1

    def straight():
        row = jnp.concatenate([half_tokens, context0, meta], axis=1)
        fill = chooser(device_count * slot_cap, slot)
        blocks = row.shape[1] // META

        def some_columns(step, state):
            take, own = state
            begin = (blocks - 1 - step) * META
            part_of = lax.dynamic_slice_in_dim(row, begin, META, 1)
            came = across(mm(fill, part_of).astype(BF), DP, slot_cap)
            take = jnp.where(step == 0, chooser(cache_size, places(came)), take)
            return take, lax.dynamic_update_slice(own, mm(take, came).astype(BF), (0, begin))

        state = (jnp.zeros((cache_size, device_count * slot_cap), BF), jnp.zeros_like(row))
        return lax.fori_loop(0, blocks, some_columns, state)[1]

    own, marks = call(
        unpack_kernel,
        None,
        [arrived],
        (of((cache_size, arrived.shape[1]), BF), of((1, LANES), F32)),
        [],
        arrived.shape[1],
    )
    ran_out = jnp.isnan(marks[0, 0]) | jnp.isnan(leg_mark.astype(F32))
    own = lax.cond(ran_out, straight, lambda: own)
    own_part, own_meta = own[:, :wide], own[:, wide:]
    own_turns = turns_of(own_meta[:, 1].astype(F32))
    other = swap(own_part)
    lower, upper = pick(own_part, other), pick(other, own_part)
    own_tokens = jnp.concatenate([lower[:, :half_width], upper[:, :half_width]], axis=1)
    own_context0 = jnp.concatenate([lower[:, half_width:], upper[:, half_width:]], axis=1)
    own_kv0 = own_by_pieces(place, own_tokens, rows0, own_turns, pieces)
    _, own_hidden0 = finish(own_part[:, :half_width], own_context0, out0, out_bias0)
    own_kv1 = project_whole(own_hidden0, rows1, own_turns, None, gathered)

    kept_kv = pick(own_kv0, own_kv1)
    got_kv = swap(pick(own_kv1, own_kv0))
    low_kv, high_kv = pick(kept_kv, got_kv), pick(got_kv, kept_kv)
    cache = jnp.concatenate(
        [low_kv[:, :part], high_kv[:, :part], low_kv[:, part:], high_kv[:, part:]], axis=1
    )
    hidden = pick(hidden0, hidden1).reshape(1, micro_count, row_count, width)
    return hidden, cache[None]


def solution(mesh):
    torus = Mesh(mesh.devices.reshape(2, 4, 4, 8), ("pipe", *DP))
    placed = (
        P(None, DP, None),
        P(None, DP),
        P(None, DP),
        P("pipe", None),
        P("pipe", None),
        P("pipe", DP, None),
        P("pipe", None),
        P("pipe", DP, None),
        P("pipe", None),
    )
    return jax.shard_map(
        shards,
        mesh=torus,
        in_specs=placed,
        out_specs=(P("pipe", None, DP, None), P("pipe", DP, None)),
        check_vma=False,
    )
```

```python
import functools

import jax
import jax.numpy as jnp
from jax import lax
from jax.experimental import pallas as pl
from jax.experimental.pallas import tpu as pltpu
from jax.sharding import Mesh
from jax.sharding import PartitionSpec as P

HDIM = 256
ROT = 64
HALF = ROT // 2
EPS = 1e-05
META = 128
LANES = 128
TILE = 256
BF = jnp.bfloat16
F32 = jnp.float32
DP = ("x", "y", "z")
PLANE = ("x", "y")
CAP_Z = 48
CAP_P = 32


def swap(value):
    return lax.ppermute(value, "pipe", [(0, 1), (1, 0)])


def mm(a, b):
    return jnp.dot(a, b, preferred_element_type=F32)


def chooser(count, places):
    return (jnp.arange(count, dtype=jnp.int32)[:, None] == places[None, :]).astype(BF)


def slots_of(dest, valid, count, cap):
    rows = dest.shape[0]
    hits = ((dest[:, None] == jnp.arange(count, dtype=jnp.int32)[None, :]) & valid[:, None]).astype(BF)
    number = jnp.arange(rows, dtype=jnp.int32)
    before = mm((number[None, :] < number[:, None]).astype(BF), hits)
    rank = jnp.sum(before * hits.astype(F32), axis=1).astype(jnp.int32)
    fits = valid & (rank < cap)
    return jnp.where(fits, dest * cap + rank, -1), jnp.any(valid & (rank >= cap))


def across(filled, axes, cap):
    cols = filled.shape[1]
    arrived = lax.all_to_all(
        filled.reshape(-1, cap, cols), axes, split_axis=0, concat_axis=0, tiled=True
    )
    return arrived.reshape(-1, cols)


def turns_of(positions):
    lane = jnp.arange(LANES)
    inverse = 10000.0 ** (-2.0 * (lane % HALF).astype(F32) / ROT)
    angles = positions[:, None] * inverse[None, :]
    cosine, sine = jnp.cos(angles), jnp.sin(angles)
    rotated, first = (lane < ROT)[None, :], (lane < HALF)[None, :]
    return jnp.stack(
        [
            jnp.where(rotated, cosine, 1.0),
            jnp.where(first, -sine, 0.0),
            jnp.where(rotated & ~first, sine, 0.0),
        ]
    )


def layer_norm(layer_in, gain_row, shift_row):
    data = layer_in.astype(F32)
    centre = jnp.mean(data, axis=-1, keepdims=True)
    centred = data - centre
    variance = jnp.mean(centred * centred, axis=-1, keepdims=True)
    return (centred * lax.rsqrt(variance + EPS) * gain_row + shift_row).astype(BF)


def rotary(cols, turns):
    parts = []
    for first in range(0, cols.shape[1], HDIM):
        head = cols[:, first : first + LANES]
        parts.append(
            head * turns[0]
            + pltpu.roll(head, LANES - HALF, 1) * turns[1]
            + pltpu.roll(head, HALF, 1) * turns[2]
        )
        parts.append(cols[:, first + LANES : first + HDIM])
    return jnp.concatenate(parts, axis=1).astype(BF)


def attend(queries, key_rows, value_rows, allowed):
    parts = []
    for first in range(0, queries.shape[1], HDIM):
        one = slice(first, first + HDIM)
        scores = lax.dot_general(
            queries[:, one], key_rows[:, one], (((1,), (1,)), ((), ())), preferred_element_type=F32
        ) * HDIM ** (-0.5)
        scores = jnp.where(allowed > 0, scores, -1e30)
        exp_scores = jnp.exp(scores - jnp.max(scores, axis=-1, keepdims=True))
        probs = (exp_scores / jnp.sum(exp_scores, axis=-1, keepdims=True)).astype(BF)
        parts.append(mm(probs, value_rows[:, one]).astype(BF))
    return jnp.concatenate(parts, axis=1)


def conclude(projected, turns, allowed_ref, out_ref):
    turns = [turns[k] for k in range(3)]
    if allowed_ref is None:
        half = projected.shape[1] // 2
        out_ref[:, :half] = rotary(projected[:, :half], turns)
        out_ref[:, half:] = projected[:, half:].astype(BF)
    else:
        third = projected.shape[1] // 3
        queries = rotary(projected[:, :third], turns)
        key_rows = rotary(projected[:, third : 2 * third], turns)
        value_rows = projected[:, 2 * third :].astype(BF)
        out_ref[...] = attend(queries, key_rows, value_rows, allowed_ref[...])


NEAR = ((0, 0, 4), (1, 0, 4), (3, 0, 4))
FAR = ((2, 0, 2), (2, 2, 2))


def cut(whole, normed):
    for k in range(normed.shape[0]):
        normed[k] = whole[:, k * LANES : (k + 1) * LANES]


def add_pieces(place, normed, parts, pieces, base, total, skipped):
    def left_hand(which, k, first, count):
        blocks = []
        for j in range(first, first + count):
            x_step, y_step = (k, j) if which == 0 else (j, k)
            x = lax.rem(place[0] + x_step, 4)
            y = lax.rem(place[1] + y_step, 4)
            blocks.append(normed[x * 4 + y])
        return jnp.concatenate(blocks, axis=1)

    def tile(which, number):
        column = pl.ds(pl.multiple_of(number * TILE, TILE), TILE)
        of_ring = pieces[len(parts) * which : len(parts) * (which + 1)]
        target = pl.ds(pl.multiple_of((3 * which + number) * TILE - skipped, TILE), TILE)
        result = jnp.broadcast_to(base[:, target], (total.shape[0], TILE))
        for part, piece in zip(parts, of_ring):
            result = result + mm(left_hand(which, *part), piece[:, column])
        total[:, target] = result

    for which in range(2):
        pl.loop(0 if which else skipped // TILE, 3)(functools.partial(tile, which))


def near_kernel(place, layer_in, gain, shift, bias, *rest):
    pieces, total, normed = rest[:-2], rest[-2], rest[-1]
    cut(layer_norm(layer_in[...], gain[...], shift[...]), normed)
    add_pieces(place, normed, NEAR, pieces, bias, total, 0)


def far_kernel(place, normed, near, turns, allowed, *rest):
    pieces, out_ref, total = rest[:-2], rest[-2], rest[-1]
    add_pieces(place, normed, FAR, pieces, near, total, 0)
    conclude(total[...], turns, allowed, out_ref)


def own_kernel(place, layer_in, gain, shift, bias, turns, *rest):
    pieces, out_ref, normed, total = rest[:-3], rest[-3], rest[-2], rest[-1]
    cut(layer_norm(layer_in[...], gain[...], shift[...]), normed)
    add_pieces(place, normed, NEAR + FAR, pieces, bias, total, 2 * TILE)
    conclude(total[...], turns, None, out_ref)


def unpack_kernel(came, own, marks):
    blocks = came.shape[1] // LANES
    last = came[:, (blocks - 1) * LANES :].astype(F32)
    lane = lax.broadcasted_iota(jnp.int32, last.shape, 1)
    named = jnp.sum(jnp.where(lane == 0, last, 0.0), axis=1, keepdims=True)
    take = (lane.astype(F32) + 1.0 == named).astype(BF)
    for first in range(0, blocks * LANES, 4 * LANES):
        part = came[:, first : min(first + 4 * LANES, blocks * LANES)]
        own[:, first : first + part.shape[1]] = lax.dot_general(
            take, part, (((0,), (0,)), ((), ())), preferred_element_type=F32
        ).astype(BF)
    marks[...] = jnp.sum(came[:, 8 * LANES : 9 * LANES].astype(F32), axis=0, keepdims=True)


def whole_kernel(with_context, layer_in, gain, shift, bias, turns, *rest):
    allowed, rest = (rest[0], rest[1:]) if with_context else (None, rest)
    weights, out_ref, normed, total = rest[:-3], rest[-3], rest[-2], rest[-1]
    step = pl.program_id(0)
    depth = weights[0].shape[0]

    @pl.when(step == 0)
    def _():
        whole = layer_norm(layer_in[...], gain[...], shift[...])
        for k in range(normed.shape[0]):
            normed[k] = whole[:, k * depth : (k + 1) * depth]
        total[...] = jnp.broadcast_to(bias[...], total.shape)

    part = normed[step]
    first = 0
    for one in weights:
        width = one.shape[1]
        total[:, first : first + width] += mm(part, one[...])
        first += width

    @pl.when(step == pl.num_programs(0) - 1)
    def _():
        conclude(total[...], turns, allowed, out_ref)


def slots_kernel(cap, meta, send, context, choice, filled, flag):
    info = meta[...].astype(F32)
    lane = lax.broadcasted_iota(jnp.int32, info.shape, 1)

    def column(k):
        return jnp.sum(jnp.where(lane == k, info, 0.0), axis=1, keepdims=True)

    valid = jnp.where(column(0) > 0.0, 1.0, 0.0)
    dest = column(2)
    hits = jnp.where(lane.astype(F32) == dest, 1.0, 0.0) * valid
    square = (info.shape[0], info.shape[0])
    row = lax.broadcasted_iota(jnp.int32, square, 0)
    earlier = jnp.where(lax.broadcasted_iota(jnp.int32, square, 1) < row, 1.0, 0.0)
    before = mm(earlier.astype(BF), hits.astype(BF))
    rank = jnp.sum(before * hits, axis=1, keepdims=True)
    slot = jnp.where(rank < cap, dest * cap + rank, -1.0) * valid + (valid - 1.0)
    place = lax.broadcasted_iota(jnp.int32, choice.shape, 1).astype(F32)
    choice[...] = jnp.where(place == slot, 1.0, 0.0).astype(BF)
    over = jnp.where(rank < cap, 0.0, 1.0) * valid + column(3)
    total = jnp.sum(over, axis=0, keepdims=True)
    flag[...] = jnp.broadcast_to(total, flag.shape)
    filled[...] = (mm(send[...], context[...]) + jnp.where(total > 0.0, jnp.nan, 0.0)).astype(BF)


def cost(rows, width, cols):
    return pl.CostEstimate(flops=rows * cols, bytes_accessed=rows * cols, transcendentals=0)


def call(kernel, place, operands, out_shape, scratch, columns):
    rows = 128
    in_specs = [pl.BlockSpec(memory_space=pltpu.VMEM)] * len(operands)
    if place is not None:
        operands = [place, *operands]
        in_specs = [pl.BlockSpec(memory_space=pltpu.SMEM), *in_specs]
    return pl.pallas_call(
        kernel,
        out_shape=out_shape,
        in_specs=in_specs,
        out_specs=jax.tree.map(lambda one: pl.BlockSpec(memory_space=pltpu.VMEM), out_shape),
        scratch_shapes=[pltpu.VMEM(*one) for one in scratch],
        cost_estimate=cost(rows, rows, columns),
        compiler_params=pltpu.CompilerParams(vmem_limit_bytes=24 << 20),
    )(*operands)


def of(shape, dtype):
    return jax.ShapeDtypeStruct(shape, dtype)


def context_by_pieces(place, layer_in, vectors, turns, allowed, pieces):
    rows = layer_in.shape[0]
    columns = vectors[2].shape[1]
    sums, blocks = of((rows, columns), F32), of((16, rows, LANES), BF)
    near = [*pieces[:3], *pieces[5:8]]
    far = [*pieces[3:5], *pieces[8:]]
    total, normed = call(near_kernel, place, [layer_in, *vectors, *near], (sums, blocks), [], columns)
    return call(
        far_kernel,
        place,
        [normed, total, turns, allowed, *far],
        of((rows, 512), BF),
        [((rows, columns), F32)],
        columns,
    )


def own_by_pieces(place, layer_in, vectors, turns, pieces):
    rows = layer_in.shape[0]
    gain, shift, bias = vectors
    bias = bias[:, 512:]
    return call(
        own_kernel,
        place,
        [layer_in, gain, shift, bias, turns, *pieces],
        of((rows, 1024), BF),
        [((16, rows, LANES), BF), ((rows, 1024), F32)],
        1024,
    )


def project_whole(layer_in, vectors, turns, allowed, gathered):
    rows, width = layer_in.shape
    gain, shift, bias = vectors
    with_context = allowed is not None
    out_cols = 512 if with_context else 1024
    if not with_context:
        bias = bias[:, 512:]
    operands = [layer_in, gain, shift, bias, turns, *((allowed,) if with_context else ())]
    depth = 512
    columns = (0, 1, 2) if with_context else (1, 2)
    return pl.pallas_call(
        functools.partial(whole_kernel, with_context),
        grid=(width // depth,),
        out_shape=jax.ShapeDtypeStruct((rows, out_cols), BF),
        in_specs=[
            pl.BlockSpec(one.shape, lambda k, rank=one.ndim: (0,) * rank) for one in operands
        ]
        + [pl.BlockSpec((depth, 512), lambda k, col=col: (k, col)) for col in columns],
        out_specs=pl.BlockSpec((rows, out_cols), lambda k: (0, 0)),
        scratch_shapes=[
            pltpu.VMEM((width // depth, rows, depth), BF),
            pltpu.VMEM((rows, bias.shape[1]), F32),
        ],
        cost_estimate=cost(rows, width, bias.shape[1]),
        compiler_params=pltpu.CompilerParams(vmem_limit_bytes=24 << 20),
    )(*operands, *[pltpu.with_memory_space_constraint(gathered, pltpu.HBM)] * len(columns))


def shifted(value, axis, by):
    size = lax.axis_size(axis)
    return lax.ppermute(value, axis, [(one, (one + by) % size) for one in range(size)])


def rings(blocks, axes, halves, later=()):
    size = lax.axis_size(axes[0])
    found = [{0: [block]} for block in blocks]
    ups = downs = list(blocks)
    for step in range(1, size // 2):
        ups = [shifted(up, axis, 1) for up, axis in zip(ups, axes)]
        downs = [shifted(down, axis, -1) for down, axis in zip(downs, axes)]
        ups, downs, later = lax.optimization_barrier((ups, downs, later))
        for one, up, down in zip(found, ups, downs):
            one[size - step], one[step] = [up], [down]
    for one, up, down, axis in zip(found, ups, downs, axes):
        rows = up.shape[0] // 2
        if halves:
            one[size // 2] = [shifted(up[:rows], axis, 1), shifted(down[rows:], axis, -1)]
        else:
            one[size // 2] = [shifted(up, axis, 1)]
    return [[one[k] for k in range(size)] for one in found], later


def column_of(shard):
    size, index = lax.axis_size("z"), lax.axis_index("z")
    block, step = shard[None], size // 2
    while step:
        got = lax.ppermute(block, "z", [(one, one ^ step) for one in range(size)])
        upper = (index // step) % 2 == 1
        both = [jnp.where(upper, got, block), jnp.where(upper, block, got)]
        block = jnp.stack(both, axis=1).reshape(-1, *shard.shape)
        step //= 2
    return block.reshape(-1, shard.shape[1])


def pieces_of(ring, later):
    half = ring.shape[1] // 2
    pair, later = rings([ring[:, :half], ring[:, half:]], ["y", "x"], False, later)
    pair = [jnp.concatenate([one[0] for one in each], axis=0) for each in pair]
    pair = lax.optimization_barrier(pair)
    order = []
    for each in rings(pair, ["x", "y"], True)[0]:
        order += [*each[0], *each[1], *each[3], *each[2]]
    return order, later


def shards(
    tokens, seg_ids, cache_row, ln_gain, ln_bias, qkv_weight, qkv_bias, out_weight, out_bias
):
    micro_count, row_count, width = tokens.shape
    device_count = lax.axis_size(DP)
    first_core = lax.axis_index("pipe") == 0
    cache_size = micro_count * row_count
    slot_cap = 2 * micro_count * ((row_count + device_count - 1) // device_count)
    head_width = qkv_weight.shape[2] // 3
    part = head_width // 2
    half_width = width // 2

    def pick(a, b):
        return jnp.where(first_core, a, b)

    def joined(piece):
        other = swap(piece)
        return jnp.concatenate([pick(piece, other), pick(other, piece)], axis=1)

    def packed(which):
        cuts = [
            qkv_weight[0][:, kind * head_width + which * part : kind * head_width + (which + 1) * part]
            for kind in range(3)
        ]
        begin = which * half_width
        out_cut = jnp.concatenate(
            [out_weight[0][:, begin : begin + part], out_weight[0][:, begin + part : begin + 2 * part]],
            axis=0,
        )
        return jnp.concatenate([*cuts, out_cut], axis=1)

    low, high = packed(0), packed(1)
    kept = pick(low, high)
    got = swap(pick(high, low))
    shard0, shard1 = pick(kept, got), pick(got, kept)
    bulk = jnp.concatenate([shard1, shard0[:, 3 * part :]], axis=1)
    gathered = lax.all_gather(bulk, DP, axis=0, tiled=True)
    pieces, (tokens, seg_ids, cache_row, ln_gain) = pieces_of(
        column_of(shard0[:, : 3 * part]), (tokens, seg_ids, cache_row, ln_gain)
    )

    vectors = jnp.concatenate([ln_gain[0], ln_bias[0], qkv_bias[0], out_bias[0]])
    vectors_got = swap(vectors)

    def vectors_of(layer):
        vec = pick(vectors, vectors_got) if layer == 0 else pick(vectors_got, vectors)
        rest = vec[2 * width :]
        bias = [
            pick(
                rest[kind * head_width : kind * head_width + part],
                rest[kind * head_width + part : (kind + 1) * head_width],
            )
            for kind in range(3)
        ]
        out_b = rest[3 * head_width :]
        rows = (vec[None, :width], vec[None, width : 2 * width], jnp.concatenate(bias)[None, :])
        return rows, pick(out_b[:half_width], out_b[half_width:])

    (rows0, out_bias0), (rows1, out_bias1) = vectors_of(0), vectors_of(1)

    flat = tokens.reshape(cache_size, width)
    seg = seg_ids.reshape(cache_size)
    rows = cache_row.reshape(cache_size)
    order = jnp.arange(cache_size, dtype=jnp.int32)
    micro = order // row_count
    same_micro = micro[:, None] == micro[None, :]
    positions = (order % row_count) - jnp.sum(
        (same_micro & (seg[None, :] < seg[:, None])).astype(jnp.int32), axis=1
    )
    earlier = order[None, :] <= order[:, None]
    allowed = (same_micro & earlier & (seg[:, None] == seg[None, :])).astype(F32)
    owners = rows // cache_size
    rank = jnp.sum(
        (same_micro & earlier & (owners[:, None] == owners[None, :])).astype(jnp.int32), axis=1
    ) - 1
    slot = owners * slot_cap + micro * (slot_cap // micro_count) + rank
    depth = lax.axis_size("z")
    lane = jnp.arange(META, dtype=jnp.int32)[None, :]
    meta = jnp.where(
        lane == 0,
        (rows % cache_size + 1)[:, None],
        jnp.where(lane == 1, positions[:, None], jnp.where(lane == 2, (owners // depth)[:, None], 0)),
    ).astype(BF)
    half_tokens = pick(flat[:, :half_width], flat[:, half_width:])
    payload = jnp.concatenate([half_tokens, meta], axis=1)
    flag_at = half_width + 3

    def flagged(filled, flag, at):
        mark = (jnp.arange(filled.shape[1]) == at).astype(BF)[None, :]
        return filled + flag.astype(BF) * mark

    slot_z, out_z = slots_of(owners % depth, rows >= 0, depth, CAP_Z)
    send_z = chooser(depth * CAP_Z, slot_z)
    filled = flagged(mm(send_z, payload).astype(BF), out_z, flag_at)
    place = jnp.stack([lax.axis_index("x"), lax.axis_index("y")]).astype(jnp.int32)
    turns = turns_of(positions.astype(F32))
    middle = across(filled, "z", CAP_Z)
    slots_p = device_count // depth * CAP_P
    context0 = context_by_pieces(place, flat, rows0, turns, allowed, pieces)
    whole = [(middle.shape[0], slots_p), (middle.shape[0], context0.shape[1]), (1, LANES)]
    send_p, filled, _ = pl.pallas_call(
        functools.partial(slots_kernel, CAP_P),
        grid=(1,),
        out_shape=(of(whole[0], BF), of(whole[1], BF), of(whole[2], F32)),
        in_specs=[
            pl.BlockSpec((middle.shape[0], META), lambda k: (0, half_width // META)),
            pl.BlockSpec(send_z.shape, lambda k: (0, 0)),
            pl.BlockSpec(context0.shape, lambda k: (0, 0)),
        ],
        out_specs=tuple(pl.BlockSpec(one, lambda k: (0, 0)) for one in whole),
        cost_estimate=cost(128, 128, 128),
    )(middle, send_z, context0)
    middle0 = across(filled, "z", CAP_Z)
    leg = jnp.concatenate([middle[:, :half_width], middle0, middle[:, half_width:]], axis=1)
    leg = lax.dot_general(
        send_p, leg, (((0,), (0,)), ((), ())), preferred_element_type=F32
    ).astype(BF)
    wide = half_width + part
    arrived = across(leg, PLANE, CAP_P)
    gathered, leg_mark, rows1, out_bias0, out_bias1 = lax.optimization_barrier(
        (gathered, leg[0, half_width], rows1, out_bias0, out_bias1)
    )

    def finish(half, context, out, out_b):
        done = jnp.concatenate([mm(context, one) for one in out], axis=1)
        done = (half.astype(F32) + done + out_b).astype(BF)
        return done, joined(done)

    def out_of(begin):
        cut = gathered[:, begin : begin + part].reshape(device_count, 2, -1, part)
        return [cut[:, k].reshape(head_width, part) for k in range(2)]

    out0, out1 = out_of(4 * part), out_of(3 * part)
    hidden0_half, hidden0 = finish(half_tokens, joined(context0), out0, out_bias0)
    arrived, hidden0_half = lax.optimization_barrier((arrived, hidden0_half))
    context1 = project_whole(hidden0, rows1, turns, allowed, gathered)
    _, hidden1 = finish(hidden0_half, joined(context1), out1, out_bias1)

    def places(came_meta):
        return came_meta[:, 0].astype(jnp.int32) - 1

    def straight():
        row = jnp.concatenate([half_tokens, context0, meta], axis=1)
        fill = chooser(device_count * slot_cap, slot)
        blocks = row.shape[1] // META

        def some_columns(step, state):
            take, own = state
            begin = (blocks - 1 - step) * META
            part_of = lax.dynamic_slice_in_dim(row, begin, META, 1)
            came = across(mm(fill, part_of).astype(BF), DP, slot_cap)
            take = jnp.where(step == 0, chooser(cache_size, places(came)), take)
            return take, lax.dynamic_update_slice(own, mm(take, came).astype(BF), (0, begin))

        state = (jnp.zeros((cache_size, device_count * slot_cap), BF), jnp.zeros_like(row))
        return lax.fori_loop(0, blocks, some_columns, state)[1]

    own, marks = call(
        unpack_kernel,
        None,
        [arrived],
        (of((cache_size, arrived.shape[1]), BF), of((1, LANES), F32)),
        [],
        arrived.shape[1],
    )
    ran_out = jnp.isnan(marks[0, 0]) | jnp.isnan(leg_mark.astype(F32))
    own = lax.cond(ran_out, straight, lambda: own)
    own_part, own_meta = own[:, :wide], own[:, wide:]
    own_turns = turns_of(own_meta[:, 1].astype(F32))
    other = swap(own_part)
    lower, upper = pick(own_part, other), pick(other, own_part)
    own_tokens = jnp.concatenate([lower[:, :half_width], upper[:, :half_width]], axis=1)
    own_context0 = jnp.concatenate([lower[:, half_width:], upper[:, half_width:]], axis=1)
    own_kv0 = own_by_pieces(place, own_tokens, rows0, own_turns, pieces)
    _, own_hidden0 = finish(own_part[:, :half_width], own_context0, out0, out_bias0)
    own_kv1 = project_whole(own_hidden0, rows1, own_turns, None, gathered)

    kept_kv = pick(own_kv0, own_kv1)
    got_kv = swap(pick(own_kv1, own_kv0))
    low_kv, high_kv = pick(kept_kv, got_kv), pick(got_kv, kept_kv)
    cache = jnp.concatenate(
        [low_kv[:, :part], high_kv[:, :part], low_kv[:, part:], high_kv[:, part:]], axis=1
    )
    hidden = pick(hidden0, hidden1).reshape(1, micro_count, row_count, width)
    return hidden, cache[None]


def solution(mesh):
    torus = Mesh(mesh.devices.reshape(2, 4, 4, 8), ("pipe", *DP))
    placed = (
        P(None, DP, None),
        P(None, DP),
        P(None, DP),
        P("pipe", None),
        P("pipe", None),
        P("pipe", DP, None),
        P("pipe", None),
        P("pipe", DP, None),
        P("pipe", None),
    )
    return jax.shard_map(
        shards,
        mesh=torus,
        in_specs=placed,
        out_specs=(P("pipe", None, DP, None), P("pipe", DP, None)),
        check_vma=False,
    )
```
